128 devices in a mesh: prow: 16 (over z, y_lo, core), pcol: 8 (over x, y_hi).
Axes of the slice: x: 4, y: 4 (y_hi: 2, y_lo: 2; y = y_hi * 2 + y_lo), z: 4, core: 2. Of those that a mesh axis runs over, the one named last changes fastest.
Arguments:
- grace_slab: float32 [90112, 2048], P('prow', 'pcol'), may hold values from -6 to 6
- goce_slab: float32 [90112, 2048], P('prow', 'pcol'), may hold values from -6 to 240
- grace_weight: float32 [1], replicated, may hold values from 0.8 to 1.25
- goce_weight: float32 [1], replicated, may hold values from 0.8 to 1.25
- kaula_prior: float32 [2048], P('pcol'), may hold values from 2 to 20
- row_target: int32 [90112], replicated, may hold values from 0 to 90111, as said below
- column_target: int32 [2048], replicated, may hold values from 0 to 2047, as said below
Outputs:
- factored: float32 [90112, 2048], P('prow', 'pcol')
The draws below stay inside these ranges and needn't reach their ends.
Inputs may be any that keep to these rules, and one draw needn't show every extreme that they name: `row_target`: a permutation; each aligned block of 5632 entries holds exactly 352 values in each aligned range of 5632 values. `column_target`: a permutation; each aligned block of 256 entries holds exactly 32 values in each aligned range of 256 values.
All inputs are finite; a program needn't handle non-finite values.
Results may differ from the reference program's by a relative error of at most 0.00005.
Values sent between devices are 32-bit elements; how exact they have to be, the bound alone decides.
A program may use at most 128 MiB of HBM per device.

```python
import math
import jax
import jax.numpy as jnp
from jax import lax

ORDER = 90112
SLAB = 2048
PANEL = 512
BLOCK = 128
N_PROW = 16
N_PCOL = 8


def balanced_targets(key, total, groups):
    per_group = total // groups
    per_pair = per_group // groups
    first_key, second_key = jax.random.split(key)
    source_perms = jax.vmap(lambda sub_key: jax.random.permutation(sub_key, per_group))(jax.random.split(first_key, groups))
    target_perms = jax.vmap(lambda sub_key: jax.random.permutation(sub_key, per_group))(jax.random.split(second_key, groups))
    sender = jnp.broadcast_to(jnp.arange(groups, dtype=jnp.int32)[:, None], (groups, per_group))
    slot_index = jnp.broadcast_to(jnp.arange(per_group, dtype=jnp.int32)[None, :], (groups, per_group))
    receiver = slot_index // per_pair
    position = sender * per_pair + slot_index % per_pair
    values = receiver * per_group + target_perms[receiver, position]
    target_index = sender * per_group + source_perms
    return jnp.zeros((total,), jnp.int32).at[target_index.ravel()].set(values.ravel().astype(jnp.int32))


def order_positions(amount, groups):
    storage = jnp.arange(amount, dtype=jnp.int32)
    per_group = amount // groups
    local = storage % per_group
    return (local // BLOCK * groups + storage // per_group) * BLOCK + storage % BLOCK


def draw_row_target(key, part):
    return balanced_targets(key, ORDER, N_PROW)


def draw_column_target(key, part):
    return balanced_targets(key, SLAB, N_PCOL)


def draw_goce_slab(key, part):
    noise_key, diag_key = jax.random.split(jax.random.fold_in(key, 7))
    noise = jnp.clip(jax.random.normal(noise_key, (ORDER, SLAB), jnp.float32), -6.0, 6.0)
    diag_values = jax.random.uniform(diag_key, (SLAB,), jnp.float32, 120.0, 240.0)
    rows = order_positions(ORDER, N_PROW)
    cols = order_positions(SLAB, N_PCOL)
    on_diagonal = rows[:, None] == cols[None, :]
    return jnp.where(on_diagonal, diag_values[None, :], noise).astype(jnp.float32)


def level_of(rng, shape, cuts, low, high):
    def one(dim, shards_of):
        draws = jax.random.uniform(jax.random.fold_in(jax.random.fold_in(rng, 6), dim), (shards_of,), jnp.float32, low / len(cuts), high / len(cuts))
        return jnp.repeat(jnp.exp(draws), shape[dim] // shards_of).reshape((-1,) + (1,) * (len(shape) - dim - 1))

    gain = one(*cuts[0])
    for cut in cuts[1:]:
        gain = gain * one(*cut)
    return gain


def scatter_about(stream_key, dims, width, reach, pieces=(), kind=jnp.bfloat16):
    gain = level_of(stream_key, dims, pieces, -0.22, 0.18) if pieces else 1.0
    array = jax.random.normal(stream_key, dims, jnp.float32) * width * gain
    return jnp.minimum(jnp.maximum(array, -reach), reach).astype(kind)


def setup_inputs(seed: int = 0) -> dict:
    key_list = jax.random.split(jax.random.key(seed), 8)
    grace_slab = scatter_about(key_list[0], (ORDER, SLAB), 1.0, 6.0, ((0, 16), (1, 8)), jnp.float32)
    goce_slab = draw_goce_slab(jax.random.fold_in(key_list[7], 71), 0)
    grace_weight = jnp.clip(jnp.exp(jax.random.uniform(key_list[2], (1,), jnp.float32, math.log(0.8), math.log(1.25))), 0.8, 1.25)
    goce_weight = jnp.clip(jnp.exp(jax.random.uniform(key_list[3], (1,), jnp.float32, math.log(0.8), math.log(1.25))), 0.8, 1.25)
    kaula_prior = jnp.clip(jnp.exp(math.log(20.0) - 2.3025851 * jax.random.uniform(key_list[4], (SLAB,), jnp.float32) ** level_of(key_list[4], (SLAB,), ((0, 8),), -0.2, 0.2)), 2.0, 20.0)
    row_target = draw_row_target(jax.random.fold_in(key_list[7], 71), 0)
    column_target = draw_column_target(jax.random.fold_in(key_list[7], 71), 0)
    return dict(grace_slab=grace_slab, goce_slab=goce_slab, grace_weight=grace_weight, goce_weight=goce_weight, kaula_prior=kaula_prior, row_target=row_target, column_target=column_target)


def order_index(amount, groups, block_size):
    storage = jnp.arange(amount, dtype=jnp.int32)
    per_group = amount // groups
    device = storage // per_group
    local = storage % per_group
    return (local // block_size * groups + device) * block_size + local % block_size

def reference(grace_slab, goce_slab, grace_weight, goce_weight, kaula_prior, row_target, column_target):
    row_order = order_index(ORDER, N_PROW, BLOCK)
    col_order = order_index(SLAB, N_PCOL, BLOCK)
    row_storage = jnp.argsort(row_order).astype(jnp.int32)
    col_storage = jnp.argsort(col_order).astype(jnp.int32)
    input_rows = jnp.argsort(row_target).astype(jnp.int32)
    input_cols = jnp.argsort(column_target).astype(jnp.int32)
    moved = jnp.take(jnp.take(grace_slab, jnp.take(input_rows, row_storage), axis=0), jnp.take(input_cols, col_storage), axis=1)
    goce_order = jnp.take(jnp.take(goce_slab, row_storage, axis=0), col_storage, axis=1)
    kaula_order = jnp.take(kaula_prior, col_storage)
    combined = grace_weight[0] * moved + goce_weight[0] * goce_order
    diag_index = jnp.arange(SLAB, dtype=jnp.int32)
    combined = combined.at[diag_index, diag_index].add(kaula_order)
    diag_block = combined[:PANEL, :PANEL]
    symmetric = jnp.tril(diag_block) + jnp.tril(diag_block, -1).T
    factor = jnp.linalg.cholesky(symmetric)
    inverse = jax.scipy.linalg.solve_triangular(factor, jnp.eye(PANEL, dtype=jnp.float32), lower=True)
    factors = jnp.dot(combined[:, :PANEL], inverse.T, precision=lax.Precision.HIGHEST)
    factors = factors.at[:PANEL].set(factor)
    update = combined[:, PANEL:] - jnp.dot(factors, factors[PANEL:SLAB].T, precision=lax.Precision.HIGHEST)
    update = update.at[:PANEL].set(combined[:PANEL, PANEL:])
    result_order = jnp.concatenate([factors, update], axis=1)
    return jnp.take(jnp.take(result_order, row_order, axis=0), col_order, axis=1)
```

```python
import functools

import jax
import jax.numpy as jnp
from jax import lax
from jax.experimental import pallas as pl
from jax.experimental.pallas import tpu as pltpu
from jax.sharding import PartitionSpec as P

F32, BF16 = jnp.float32, jnp.bfloat16
MESH = pl.DeviceIdType.MESH
HIGHEST = lax.Precision.HIGHEST
PANEL, BLOCK = 512, 128
NPR, NPC = 16, 8
RH, CH = 5632, 256
GR, GC = RH // NPR, CH // NPC
QR = GR // 4
CR = 256
NC = RH // CR
VMEM_LIMIT = 60 * 2**20


def iota(shape, dim):
    return lax.broadcasted_iota(jnp.int32, shape, dim)


def select_columns(values, onehot):
    high = values.astype(BF16)
    rest = values - high.astype(F32)
    middle = rest.astype(BF16)
    low = (rest - middle.astype(F32)).astype(BF16)
    dot = functools.partial(jnp.dot, preferred_element_type=F32)
    return dot(high, onehot) + dot(middle, onehot) + dot(low, onehot)


def regroup(parts, lane):
    results = []
    for m in range(4):
        joined = None
        for k in range(4):
            moved = parts[k] if k == m else pltpu.roll(parts[k], ((k - m) * GC) % 128, 1)
            joined = moved if k == 0 else jnp.where(lane // GC == k, moved, joined)
        results.append(joined)
    return results


def pack_kernel(order, col_down, col_across, x, out, rows, onehot):
    part = pl.program_id(0)

    @pl.when(part == 0)
    def _():
        below = (col_down[...] > col_across[...]).astype(F32)
        rank = jnp.sum(below, axis=1, keepdims=True).astype(jnp.int32)
        onehot[...] = jnp.where(rank == iota((CH, CH), 1), 1.0, 0.0).astype(BF16)

    base = part * GR

    def gather(i, carry):
        for u in range(8):
            rows[i, u : u + 1, :] = x[pl.ds(order[base + i * 8 + u], 1), :]
        return carry

    lax.fori_loop(0, GR // 8, gather, 0)
    picked = select_columns(rows[...].reshape(GR, CH), onehot[...])
    lane = iota((QR, 128), 1)
    for half in range(2):
        parts = [picked[g * QR : (g + 1) * QR, half * 128 : half * 128 + 128] for g in range(4)]
        for q, joined in enumerate(regroup(parts, lane)):
            out[half * 4 + q] = joined


def pack(order, col_targets, x):
    return pl.pallas_call(
        pack_kernel,
        out_shape=jax.ShapeDtypeStruct((NPR * NPC, QR, 128), F32),
        grid_spec=pltpu.PrefetchScalarGridSpec(
            num_scalar_prefetch=1,
            grid=(NPR,),
            in_specs=[
                pl.BlockSpec((CH, 1), lambda i, o: (0, 0)),
                pl.BlockSpec((1, CH), lambda i, o: (0, 0)),
                pl.BlockSpec((RH, CH), lambda i, o: (0, 0), pipeline_mode=pl.Buffered(1)),
            ],
            out_specs=pl.BlockSpec((NPC, QR, 128), lambda i, o: (i, 0, 0)),
            scratch_shapes=[pltpu.VMEM((GR // 8, 8, CH), F32), pltpu.VMEM((CH, CH), BF16)],
        ),
        compiler_params=pltpu.CompilerParams(vmem_limit_bytes=VMEM_LIMIT),
        name="pack",
    )(order, col_targets.reshape(CH, 1), col_targets.reshape(1, CH), x)


OUT_ROWS = 512


def unpack_kernel(place, weights, col_all, kaula, received, goce, out, moved, rows, onehot):
    step = pl.program_id(0)
    row_id, col_id = lax.axis_index("prow"), lax.axis_index("pcol")

    @pl.when(step == 0)
    def _():
        source = jnp.zeros((CH, 128), F32)
        here = col_id * CH + iota((CH, 128), 0)
        for r in range(16):
            source += jnp.where(col_all[r : r + 1, :] == here, float(r // 2), 0.0)
        source = jnp.sum(source, axis=1, keepdims=True)
        across = jnp.transpose(jnp.broadcast_to(source, (CH, 128)))[0:1, :]
        earlier = (source == across) & (iota((CH, CH), 0) < iota((CH, CH), 1))
        rank = jnp.sum(jnp.where(earlier, 1.0, 0.0), axis=0, keepdims=True)
        arrival = (across * GC + rank).astype(jnp.int32)
        onehot[...] = jnp.where(iota((CH, CH), 0) == arrival, 1.0, 0.0).astype(BF16)

    @pl.when(step < NPR)
    def _():
        lane = iota((QR, 128), 1)
        halves = [regroup([received[h * 4 + q] for q in range(4)], lane) for h in range(2)]
        joined = jnp.concatenate(
            [jnp.concatenate([halves[0][g], halves[1][g]], axis=1) for g in range(4)], axis=0
        )
        rows[...] = select_columns(joined, onehot[...]).reshape(GR // 8, 8, CH)
        base = step * GR

        def scatter(i, carry):
            for u in range(8):
                moved[pl.ds(place[base + i * 8 + u], 1), :] = rows[i, u : u + 1, :]
            return carry

        lax.fori_loop(0, GR // 8, scatter, 0)

    @pl.when(step >= NPR)
    def _():
        part = step - NPR
        first = pl.multiple_of(part * OUT_ROWS, OUT_ROWS)
        out[...] = weights[0] * moved[pl.ds(first, OUT_ROWS), :] + weights[1] * goce[...]

    @pl.when((step == NPR) & (row_id % NPC == col_id))
    def _():
        equal = iota((BLOCK, BLOCK), 0) == iota((BLOCK, BLOCK), 1)
        for half in range(2):
            cols = slice(half * BLOCK, (half + 1) * BLOCK)
            add = jnp.where(equal & (row_id // NPC == half), kaula[:, cols], 0.0)
            out[:BLOCK, cols] = out[:BLOCK, cols] + add


def unpack(place, weights, col_all, kaula, received, goce):
    return pl.pallas_call(
        unpack_kernel,
        out_shape=jax.ShapeDtypeStruct((RH, CH), F32),
        grid_spec=pltpu.PrefetchScalarGridSpec(
            num_scalar_prefetch=2,
            grid=(NPR + RH // OUT_ROWS,),
            in_specs=[
                pl.BlockSpec((16, 128), lambda i, *_: (0, 0)),
                pl.BlockSpec((1, CH), lambda i, *_: (0, 0)),
                pl.BlockSpec((NPC, QR, 128), lambda i, *_: (jnp.minimum(i, NPR - 1), 0, 0)),
                pl.BlockSpec((OUT_ROWS, CH), lambda i, *_: (jnp.maximum(i - NPR, 0), 0)),
            ],
            out_specs=pl.BlockSpec((OUT_ROWS, CH), lambda i, *_: (jnp.maximum(i - NPR, 0), 0)),
            scratch_shapes=[
                pltpu.VMEM((RH, CH), F32),
                pltpu.VMEM((GR // 8, 8, CH), F32),
                pltpu.VMEM((CH, CH), BF16),
            ],
        ),
        compiler_params=pltpu.CompilerParams(vmem_limit_bytes=VMEM_LIMIT),
        name="unpack",
    )(place, weights, col_all.reshape(16, 128), kaula.reshape(1, CH), received, goce)


def eliminate(group, carry, factor_t, inverse):
    d, x = list(carry[:16]), list(carry[16:])
    lane, sub = iota((8, 128), 1), iota((8, 128), 0)
    f_rows = jnp.zeros((8, 128), F32)
    x_rows = jnp.zeros((8, 128), F32)
    live = lane < 128 - 8 * group
    for s in range(8):
        row = jnp.broadcast_to(d[0][s : s + 1, :], (8, 128))
        pivot = jnp.broadcast_to(row[:, s : s + 1], (8, 128))
        r = lax.rsqrt(pivot)
        r = r * (1.5 - 0.5 * pivot * r * r)
        row = jnp.where(live & (lane >= s), row, 0.0) * r
        x_row = jnp.broadcast_to(x[0][s : s + 1, :], (8, 128)) * r
        f_rows = jnp.where(sub == s, row, f_rows)
        x_rows = jnp.where(sub == s, x_row, x_rows)
        row, x_row = row * r, x_row * r
        for i in range(16):
            column = jnp.broadcast_to(d[i][:, s : s + 1], (8, 128))
            d[i] = d[i] - column * row
            x[i] = x[i] - column * x_row
        d[0] = jnp.where(sub == s, 0.0, d[0])
    at = pl.ds(pl.multiple_of(group * 8, 8), 8)
    factor_t[at, :] = pltpu.roll(f_rows, group * 8, 1)
    inverse[at, :] = x_rows
    d = [pltpu.roll(v, 120, 1) for v in d[1:] + d[:1]]
    return tuple(d + x[1:] + x[:1])


def panel_kernel(
    a_hbm, out, a, panel, heads, work, factor_t, w_high, w_low, diag_f, diag_x,
    load, sent0, got0, sent1, got1, sent2, got2, head_sent, head_got,
):
    row_id, col_id = lax.axis_index("prow"), lax.axis_index("pcol")
    cx, cy = col_id // 2, col_id % 2
    cz, cyc = row_id // 4, row_id % 4
    left = cx < 2
    b = jnp.where(left, cx, 3 - cx)
    own = b * 2 + cy
    cross = (row_id, (3 - cx) * 2 + cy)
    x_mate = (row_id, (cx + 1 - 2 * (cx % 2)) * 2 + cy)
    y_mate = (row_id, cx * 2 + 1 - cy)
    over_z = [(lax.rem(cz + k, 4) * 4 + cyc, col_id) for k in (1, 2, 3)]
    in_z = [(cz * 4 + lax.rem(cyc + k, 4), col_id) for k in (1, 2, 3)]

    @pl.when(left)
    def _():
        pltpu.make_async_copy(a_hbm.at[:, pl.ds(0, BLOCK)], panel.at[own], load.at[0]).start()

    pltpu.make_async_copy(a_hbm, a, load.at[1]).start()
    barrier = pltpu.get_barrier_semaphore()
    for device in [cross, x_mate, y_mate] + over_z + in_z:
        pl.semaphore_signal(barrier, inc=1, device_id=device, device_id_type=MESH)
    pl.semaphore_wait(barrier, 9)

    @pl.when(left)
    def _():
        pltpu.make_async_copy(a_hbm.at[:, pl.ds(0, BLOCK)], panel.at[own], load.at[0]).wait()

    def piece(j, c):
        return panel.at[j, pl.ds(c * CR, CR), :]

    def send(j, c, sent, got, device):
        return pltpu.make_async_remote_copy(
            piece(j, c), piece(j, c), sent, got, device_id=device, device_id_type=MESH
        )

    flip_x, flip_y = (1 - b) * 2 + cy, b * 2 + 1 - cy
    flip_both = (1 - b) * 2 + 1 - cy

    def plan(c):
        if c % 2 == 0:
            return x_mate, flip_x, y_mate, flip_y
        return y_mate, flip_y, x_mate, flip_x

    def start0(c):
        @pl.when(left)
        def _():
            send(own, c, sent0.at[c], got0.at[c], cross).start()

    def start1(c):
        @pl.when(jnp.logical_not(left))
        def _():
            send(own, c, sent0.at[c], got0.at[c], cross).wait_recv()

        send(own, c, sent1.at[c], got1.at[c], plan(c)[0]).start()

    def start2(c):
        mate1, j1, mate2, _ = plan(c)
        send(j1, c, sent1.at[c], got1.at[c], mate1).wait_recv()
        send(own, c, sent2.at[c, 0], got2.at[c, 0], mate2).start()
        send(j1, c, sent2.at[c, 1], got2.at[c, 1], mate2).start()

    def finish2(c):
        _, _, mate2, j2 = plan(c)
        send(j2, c, sent2.at[c, 0], got2.at[c, 0], mate2).wait_recv()
        send(flip_both, c, sent2.at[c, 1], got2.at[c, 1], mate2).wait_recv()

    ahead0, ahead1 = 6, 3

    def tick(t):
        if t + ahead0 < NC:
            start0(t + ahead0)
        if t + ahead1 < NC:
            start1(t + ahead1)
        if t < NC:
            start2(t)

    for c in range(ahead0):
        start0(c)
    for c in range(ahead1):
        start1(c)

    head = panel.at[:, pl.ds(0, BLOCK), :]
    a_owner = cyc == col_id % 4
    first_z = col_id // 4

    def head_local(slot):
        return pltpu.make_async_copy(head, heads.at[slot], head_got.at[slot])

    def head_copy(source, slot, k, base, device):
        return pltpu.make_async_remote_copy(
            source, heads.at[slot], head_sent.at[base + k], head_got.at[slot],
            device_id=device, device_id_type=MESH,
        )

    sources = [(cz == 0, cyc, 0), (a_owner & (cz == first_z), 4, 3), (a_owner & (cz == first_z + 2), 5, 6)]

    def head_out():
        for mine, slot, base in sources:

            @pl.when(mine)
            def _(slot=slot, base=base):
                head_local(slot).start()
                for k in range(3):
                    head_copy(head, slot, k, base, over_z[k]).start()

    def head_spread():
        head_local(cyc).wait()
        for k in range(3):
            head_copy(heads.at[cyc], cyc, k, 9, in_z[k]).start()

        @pl.when(a_owner)
        def _():
            for slot, base in ((4, 12), (5, 15)):
                head_local(slot).wait()
                for k in range(3):
                    head_copy(heads.at[slot], slot, k, base, in_z[k]).start()

    def head_in():
        for k in (1, 2, 3):
            head_local(lax.rem(cyc + k, 4)).wait()

        @pl.when(jnp.logical_not(a_owner))
        def _():
            for slot in (4, 5):
                head_local(slot).wait()

    def head_done():
        for mine, slot, base in sources:

            @pl.when(mine)
            def _(slot=slot, base=base):
                for k in range(3):
                    head_copy(head, slot, k, base, over_z[k]).wait_send()

        for k in range(3):
            head_copy(heads.at[cyc], cyc, k, 9, in_z[k]).wait_send()

        @pl.when(a_owner)
        def _():
            for slot, base in ((4, 12), (5, 15)):
                for k in range(3):
                    head_copy(heads.at[slot], slot, k, base, in_z[k]).wait_send()

    t = 0

    def advance():
        nonlocal t
        tick(t)
        t += 1

    advance()
    advance()
    finish2(0)
    head_out()
    advance()
    advance()
    head_spread()
    advance()
    advance()
    head_in()

    lower = iota((BLOCK, BLOCK), 0) >= iota((BLOCK, BLOCK), 1)
    for i in range(4):
        rows = slice(i * BLOCK, (i + 1) * BLOCK)
        for j in range(i):
            block = heads[i, j]
            work[rows, j * BLOCK : (j + 1) * BLOCK] = block
            work[j * BLOCK : (j + 1) * BLOCK, rows] = jnp.transpose(block)
        block = heads[i, i]
        work[rows, rows] = jnp.where(lower, block, jnp.transpose(block))
        for j in range(4):
            unit = jnp.where(iota((BLOCK, BLOCK), 0) == iota((BLOCK, BLOCK), 1), float(i == j), 0.0)
            work[rows, PANEL + j * BLOCK : PANEL + (j + 1) * BLOCK] = unit
            factor_t[rows, j * BLOCK : (j + 1) * BLOCK] = jnp.zeros((BLOCK, BLOCK), F32)

    for k in range(4):
        rows = slice(k * BLOCK, (k + 1) * BLOCK)
        carry = [work[k * BLOCK + g * 8 : k * BLOCK + g * 8 + 8, rows] for g in range(16)]
        carry += [
            work[k * BLOCK + g * 8 : k * BLOCK + g * 8 + 8, PANEL + k * BLOCK : PANEL + (k + 1) * BLOCK]
            for g in range(16)
        ]
        carry = tuple(carry)
        for part in range(4):
            carry = lax.fori_loop(
                part * 4, part * 4 + 4, lambda g, v: eliminate(g, v, diag_f, diag_x), carry
            )
            if part % 2:
                advance()
        factor_t[rows, rows] = diag_f[...]
        right = (k + 1) * BLOCK
        width = PANEL + (k + 1) * BLOCK - right
        solved = jnp.dot(diag_x[...], work[rows, right : right + width], precision=HIGHEST)
        work[rows, right : right + width] = solved
        count = PANEL - right
        if count:
            factor_t[rows, right:PANEL] = solved[:, :count]
            turned = jnp.transpose(solved[:, :count])
            work[right:PANEL, right : right + width] -= jnp.dot(turned, solved, precision=HIGHEST)
        advance()

    columns = jnp.concatenate(
        [jnp.concatenate([heads[4 + i, j] for j in range(4)], axis=1) for i in range(2)], axis=0
    )
    solved = lax.dot_general(
        work[:, PANEL:], columns, (((1,), (1,)), ((), ())), precision=HIGHEST, preferred_element_type=F32
    )
    turned = jnp.transpose(work[:, PANEL:])
    weight = jnp.dot(turned, solved, precision=HIGHEST)
    work[:, :PANEL] = turned
    own_panel = col_id < PANEL // BLOCK
    direct = -work[:, pl.ds(pl.multiple_of(jnp.minimum(col_id, 3) * BLOCK, BLOCK), BLOCK)]
    weight = jnp.concatenate([jnp.where(own_panel, direct, weight[:, :BLOCK]), weight[:, BLOCK:]], axis=1)
    high = weight.astype(BF16)
    w_high[...] = high
    w_low[...] = (weight - high.astype(F32)).astype(BF16)
    while t < NC:
        advance()

    pltpu.make_async_copy(a_hbm, a, load.at[1]).wait()
    in_panel = iota((CR, CH), 1) < jnp.where(own_panel, BLOCK, 0)
    dot = functools.partial(jnp.dot, preferred_element_type=F32)
    for c in range(NC):
        if c:
            finish2(c)
        at = slice(c * CR, (c + 1) * CR)
        left_rows = jnp.concatenate([panel[j, at, :] for j in range(4)], axis=1)
        high = left_rows.astype(BF16)
        low = (left_rows - high.astype(F32)).astype(BF16)
        update = dot(high, w_high[...]) + (dot(high, w_low[...]) + dot(low, w_high[...]))
        out[at, :] = jnp.where(in_panel, 0.0, a[at, :]) - update
        if c == 0:

            @pl.when(row_id < PANEL // BLOCK)
            def _():
                d, j = jnp.minimum(row_id, 3), jnp.minimum(col_id, 3)
                block = factor_t[
                    pl.ds(pl.multiple_of(j * BLOCK, BLOCK), BLOCK), pl.ds(pl.multiple_of(d * BLOCK, BLOCK), BLOCK)
                ]
                out[:BLOCK, :BLOCK] = jnp.where(own_panel, jnp.transpose(block), a[:BLOCK, :BLOCK])
                out[:BLOCK, BLOCK:] = a[:BLOCK, BLOCK:]

    for c in range(NC):

        @pl.when(left)
        def _(c=c):
            send(own, c, sent0.at[c], got0.at[c], cross).wait_send()

        mate1, j1, mate2, _ = plan(c)
        send(own, c, sent1.at[c], got1.at[c], mate1).wait_send()
        send(own, c, sent2.at[c, 0], got2.at[c, 0], mate2).wait_send()
        send(j1, c, sent2.at[c, 1], got2.at[c, 1], mate2).wait_send()
    head_done()


def panel_step(combined):
    dma = pltpu.SemaphoreType.DMA
    return pl.pallas_call(
        panel_kernel,
        out_shape=jax.ShapeDtypeStruct((RH, CH), F32),
        in_specs=[pl.BlockSpec(memory_space=pl.ANY)],
        out_specs=pl.BlockSpec(memory_space=pltpu.VMEM),
        scratch_shapes=[
            pltpu.VMEM((RH, CH), F32),
            pltpu.VMEM((4, RH, BLOCK), F32),
            pltpu.VMEM((6, 4, BLOCK, BLOCK), F32),
            pltpu.VMEM((PANEL, 2 * PANEL), F32),
            pltpu.VMEM((PANEL, PANEL), F32),
            pltpu.VMEM((PANEL, CH), BF16),
            pltpu.VMEM((PANEL, CH), BF16),
            pltpu.VMEM((BLOCK, BLOCK), F32),
            pltpu.VMEM((BLOCK, BLOCK), F32),
            dma((2,)),
            dma((NC,)),
            dma((NC,)),
            dma((NC,)),
            dma((NC,)),
            dma((NC, 2)),
            dma((NC, 2)),
            dma((18,)),
            dma((6,)),
        ],
        compiler_params=pltpu.CompilerParams(
            collective_id=0, has_side_effects=True, vmem_limit_bytes=VMEM_LIMIT
        ),
        name="panel_step",
    )(combined)


def shards(grace_slab, goce_slab, grace_weight, goce_weight, kaula_prior, row_target, column_target):
    row_id, col_id = lax.axis_index("prow"), lax.axis_index("pcol")
    targets = lax.dynamic_slice_in_dim(row_target, row_id * RH, RH)
    targets, order = lax.sort((targets, jnp.arange(RH, dtype=jnp.int32)), num_keys=1)
    place = lax.all_to_all(targets.reshape(NPR, GR), "prow", split_axis=0, concat_axis=0, tiled=True)
    place = place.reshape(RH) - row_id * RH
    col_targets = lax.dynamic_slice_in_dim(column_target, col_id * CH, CH)
    packed = pack(order, col_targets, grace_slab)
    received = lax.all_to_all(packed, ("prow", "pcol"), split_axis=0, concat_axis=0, tiled=True)
    weights = jnp.concatenate([grace_weight, goce_weight])
    combined = unpack(place, weights, column_target, kaula_prior, received, goce_slab)
    return panel_step(combined)


def solution(mesh):
    return jax.shard_map(
        shards,
        mesh=mesh,
        in_specs=(P("prow", "pcol"), P("prow", "pcol"), P(), P(), P("pcol"), P(), P()),
        out_specs=P("prow", "pcol"),
        check_vma=False,
    )
```

```python
import functools

import jax
import jax.numpy as jnp
from jax import lax
from jax.experimental import pallas as pl
from jax.experimental.pallas import tpu as pltpu
from jax.sharding import PartitionSpec as P

F32, BF16 = jnp.float32, jnp.bfloat16
MESH = pl.DeviceIdType.MESH
HIGHEST = lax.Precision.HIGHEST
PANEL, BLOCK = 512, 128
NPR, NPC = 16, 8
RH, CH = 5632, 256
GR, GC = RH // NPR, CH // NPC
QR = GR // 4
CR = 256
NC = RH // CR
VMEM_LIMIT = 60 * 2**20


def iota(shape, dim):
    return lax.broadcasted_iota(jnp.int32, shape, dim)


def select_columns(values, onehot):
    high = values.astype(BF16)
    rest = values - high.astype(F32)
    middle = rest.astype(BF16)
    low = (rest - middle.astype(F32)).astype(BF16)
    dot = functools.partial(jnp.dot, preferred_element_type=F32)
    return dot(high, onehot) + dot(middle, onehot) + dot(low, onehot)


def regroup(parts, lane):
    results = []
    for m in range(4):
        joined = None
        for k in range(4):
            moved = parts[k] if k == m else pltpu.roll(parts[k], ((k - m) * GC) % 128, 1)
            joined = moved if k == 0 else jnp.where(lane // GC == k, moved, joined)
        results.append(joined)
    return results


def linear(row):
    return row // 8 * 16 + row % 8


def other_row(row_id, step, sign):
    z, y, core = row_id // 4, row_id // 2 % 2, row_id % 2
    dz, dy, dcore = step % 4, step // 4 % 2, step // 8
    return lax.rem(z + sign * dz + 4, 4) * 4 + lax.rem(y + dy, 2) * 2 + lax.rem(core + dcore, 2)


def other_col(col_id, step, sign):
    x, y = col_id // 2, col_id % 2
    return lax.rem(x + sign * (step // 2) + 4, 4) * 2 + lax.rem(y + step % 2, 2)


def exchange_kernel(
    order, col_down, col_across, col_all, places, x, out, places_out,
    rows, packed, received, pick_out, pick_in, sent, got, place_sent, place_got,
):
    row_id, col_id = lax.axis_index("prow"), lax.axis_index("pcol")
    me = row_id * NPC + col_id
    lane = iota((QR, 128), 1)

    barrier = pltpu.get_barrier_semaphore()

    def greet(k, carry):
        device = (other_row(row_id, k // NPC, 1), other_col(col_id, k % NPC, 1))
        pl.semaphore_signal(barrier, inc=1, device_id=device, device_id_type=MESH)
        return carry

    lax.fori_loop(1, NPR * NPC, greet, 0)

    below = (col_down[...] > col_across[...]).astype(F32)
    rank = jnp.sum(below, axis=1, keepdims=True).astype(jnp.int32)
    pick_out[...] = jnp.where(rank == iota((CH, CH), 1), 1.0, 0.0).astype(BF16)

    def pack(step):
        dest = other_row(row_id, step, 1)
        base = dest * GR

        def gather(i, carry):
            for u in range(16):
                at = order[base + i * 16 + u]
                tile, sub = i * 2 + u // 8, u % 8
                rows[tile, 0, sub : sub + 1, :] = x[pl.ds(at, 1), :]
                rows[tile, 1, sub : sub + 1, :] = x[pl.ds(at + 8, 1), :]
            return carry

        lax.fori_loop(0, GR // 16, gather, 0)
        taken = jnp.concatenate([rows[:, h].reshape(GR, 128) for h in range(2)], axis=1)
        picked = select_columns(taken, pick_out[...])
        for half in range(2):
            parts = [picked[g * QR : (g + 1) * QR, half * 128 : half * 128 + 128] for g in range(4)]
            for q, joined in enumerate(regroup(parts, lane)):
                packed[dest * NPC + half * 4 + q] = joined

    def chunk_copy(dest_row, dest_col, source):
        to = dest_row * NPC + dest_col
        return pltpu.make_async_remote_copy(
            packed.at[to], received.at[source], sent.at[to], got.at[source],
            device_id=(dest_row, dest_col), device_id_type=MESH,
        )

    def place_copy(dest_row, source_row):
        return pltpu.make_async_remote_copy(
            places.at[dest_row], places_out.at[source_row], place_sent.at[dest_row],
            place_got.at[source_row], device_id=(dest_row, col_id), device_id_type=MESH,
        )

    def own_copy():
        return pltpu.make_async_copy(packed.at[me], received.at[me], got.at[me])

    def own_places():
        return pltpu.make_async_copy(places.at[row_id], places_out.at[row_id], place_got.at[row_id])

    pack(0)
    pl.semaphore_wait(barrier, NPR * NPC - 1)
    pack(1)
    own_copy().start()
    own_places().start()
    for k in range(1, NPC):
        chunk_copy(row_id, other_col(col_id, k, 1), me).start()

    def forward(step, carry):
        @pl.when(step < NPR - 1)
        def _():
            pack(step + 1)

        dest = other_row(row_id, step, 1)
        place_copy(dest, row_id).start()
        for k in range(NPC):
            chunk_copy(dest, other_col(col_id, k, 1), me).start()
        return carry

    lax.fori_loop(1, NPR, forward, 0)

    source = jnp.zeros((CH, 128), F32)
    here = col_id * CH + iota((CH, 128), 0)
    for r in range(16):
        source += jnp.where(col_all[r : r + 1, :] == here, float(r // 2), 0.0)
    source = jnp.sum(source, axis=1, keepdims=True)
    across = jnp.transpose(jnp.broadcast_to(source, (CH, 128)))[0:1, :]
    earlier = (source == across) & (iota((CH, CH), 0) < iota((CH, CH), 1))
    rank = jnp.sum(jnp.where(earlier, 1.0, 0.0), axis=0, keepdims=True)
    arrival = (across * GC + rank).astype(jnp.int32)
    pick_in[...] = jnp.where(iota((CH, CH), 0) == arrival, 1.0, 0.0).astype(BF16)

    def unpack(origin):
        halves = [regroup([received[origin * NPC + h * 4 + q] for q in range(4)], lane) for h in range(2)]
        joined = jnp.concatenate(
            [jnp.concatenate([halves[0][g], halves[1][g]], axis=1) for g in range(4)], axis=0
        )
        picked = select_columns(joined, pick_in[...])
        for h in range(2):
            out[origin, :, h] = picked[:, h * 128 : h * 128 + 128].reshape(GR // 8, 8, 128)

    own_copy().wait()
    own_places().wait()
    for k in range(1, NPC):
        origin = other_col(col_id, k, -1)
        chunk_copy(row_id, col_id, row_id * NPC + origin).wait_recv()
    unpack(row_id)

    def arrive(step, carry):
        origin = other_row(row_id, step, -1)
        place_copy(row_id, origin).wait_recv()
        for k in range(NPC):
            chunk_copy(row_id, col_id, origin * NPC + other_col(col_id, k, -1)).wait_recv()
        unpack(origin)
        return carry

    lax.fori_loop(1, NPR, arrive, 0)

    for k in range(1, NPC):
        chunk_copy(row_id, other_col(col_id, k, 1), me).wait_send()

    def leave(step, carry):
        dest = other_row(row_id, step, 1)
        place_copy(dest, row_id).wait_send()
        for k in range(NPC):
            chunk_copy(dest, other_col(col_id, k, 1), me).wait_send()
        return carry

    lax.fori_loop(1, NPR, leave, 0)


def exchange(order, col_targets, col_all, places, x):
    dma, vmem = pltpu.SemaphoreType.DMA, pl.BlockSpec(memory_space=pltpu.VMEM)
    return pl.pallas_call(
        exchange_kernel,
        out_shape=(
            jax.ShapeDtypeStruct((NPR, GR // 8, 2, 8, 128), F32),
            jax.ShapeDtypeStruct((NPR, 1, PLACES), jnp.int32),
        ),
        in_specs=[pl.BlockSpec(memory_space=pltpu.SMEM)] + [vmem] * 5,
        out_specs=(vmem, vmem),
        scratch_shapes=[
            pltpu.VMEM((GR // 8, 2, 8, 128), F32),
            pltpu.VMEM((NPR * NPC, QR, 128), F32),
            pltpu.VMEM((NPR * NPC, QR, 128), F32),
            pltpu.VMEM((CH, CH), BF16),
            pltpu.VMEM((CH, CH), BF16),
            dma((NPR * NPC,)),
            dma((NPR * NPC,)),
            dma((NPR,)),
            dma((NPR,)),
        ],
        compiler_params=pltpu.CompilerParams(
            collective_id=1, has_side_effects=True, vmem_limit_bytes=VMEM_LIMIT
        ),
        name="exchange",
    )(order, col_targets.reshape(CH, 1), col_targets.reshape(1, CH), col_all.reshape(16, 128), places, x)


OUT_ROWS = 512
PLACES = 384


def place_kernel(place, weights, kaula, rows, goce, out, moved):
    step = pl.program_id(0)
    row_id, col_id = lax.axis_index("prow"), lax.axis_index("pcol")

    @pl.when(step < NPR)
    def _():
        base = step * PLACES

        def scatter(i, carry):
            for u in range(16):
                at = place[base + i * 16 + u]
                tile, sub = i * 2 + u // 8, u % 8
                moved[pl.ds(at, 1), :] = rows[0, tile, 0, sub : sub + 1, :]
                moved[pl.ds(at + 8, 1), :] = rows[0, tile, 1, sub : sub + 1, :]
            return carry

        lax.fori_loop(0, GR // 16, scatter, 0)

    @pl.when(step >= NPR)
    def _():
        first = pl.multiple_of((step - NPR) * 2 * OUT_ROWS, OUT_ROWS)
        block = moved[pl.ds(first, 2 * OUT_ROWS), :].reshape(OUT_ROWS // 8, 2, 8, 128)
        for h in range(2):
            cols = slice(h * 128, h * 128 + 128)
            out[:, cols] = weights[0] * block[:, h].reshape(OUT_ROWS, 128) + weights[1] * goce[:, cols]

    @pl.when((step == NPR) & (row_id % NPC == col_id))
    def _():
        equal = iota((BLOCK, BLOCK), 0) == iota((BLOCK, BLOCK), 1)
        for half in range(2):
            cols = slice(half * BLOCK, (half + 1) * BLOCK)
            add = jnp.where(equal & (row_id // NPC == half), kaula[:, cols], 0.0)
            out[:BLOCK, cols] = out[:BLOCK, cols] + add


def place_rows(place, weights, kaula, rows, goce):
    return pl.pallas_call(
        place_kernel,
        out_shape=jax.ShapeDtypeStruct((RH, CH), F32),
        grid_spec=pltpu.PrefetchScalarGridSpec(
            num_scalar_prefetch=2,
            grid=(NPR + RH // OUT_ROWS,),
            in_specs=[
                pl.BlockSpec((1, CH), lambda i, *_: (0, 0)),
                pl.BlockSpec(
                    (1, GR // 8, 2, 8, 128), lambda i, *_: (jnp.minimum(i, NPR - 1), 0, 0, 0, 0)
                ),
                pl.BlockSpec((OUT_ROWS, CH), lambda i, *_: (jnp.maximum(i - NPR, 0), 0)),
            ],
            out_specs=pl.BlockSpec((OUT_ROWS, CH), lambda i, *_: (jnp.maximum(i - NPR, 0), 0)),
            scratch_shapes=[pltpu.VMEM((2 * RH, 128), F32)],
        ),
        compiler_params=pltpu.CompilerParams(vmem_limit_bytes=VMEM_LIMIT),
        name="place_rows",
    )(place, weights, kaula.reshape(1, CH), rows, goce)


def eliminate(group, carry, factor_t, inverse):
    d, x = list(carry[:16]), list(carry[16:])
    lane, sub = iota((8, 128), 1), iota((8, 128), 0)
    f_rows = jnp.zeros((8, 128), F32)
    x_rows = jnp.zeros((8, 128), F32)
    live = lane < 128 - 8 * group
    for s in range(8):
        row = jnp.broadcast_to(d[0][s : s + 1, :], (8, 128))
        pivot = jnp.broadcast_to(row[:, s : s + 1], (8, 128))
        r = lax.rsqrt(pivot)
        r = r * (1.5 - 0.5 * pivot * r * r)
        row = jnp.where(live & (lane >= s), row, 0.0) * r
        x_row = jnp.broadcast_to(x[0][s : s + 1, :], (8, 128)) * r
        f_rows = jnp.where(sub == s, row, f_rows)
        x_rows = jnp.where(sub == s, x_row, x_rows)
        row, x_row = row * r, x_row * r
        for i in range(16):
            column = jnp.broadcast_to(d[i][:, s : s + 1], (8, 128))
            d[i] = d[i] - column * row
            x[i] = x[i] - column * x_row
        d[0] = jnp.where(sub == s, 0.0, d[0])
    at = pl.ds(pl.multiple_of(group * 8, 8), 8)
    factor_t[at, :] = pltpu.roll(f_rows, group * 8, 1)
    inverse[at, :] = x_rows
    d = [pltpu.roll(v, 120, 1) for v in d[1:] + d[:1]]
    return tuple(d + x[1:] + x[:1])


def panel_kernel(
    a_hbm, out, a, panel, heads, work, factor_t, w_high, w_low, diag_f, diag_x,
    load, sent0, got0, sent1, got1, sent2, got2, head_sent, head_got,
):
    row_id, col_id = lax.axis_index("prow"), lax.axis_index("pcol")
    cx, cy = col_id // 2, col_id % 2
    cz, cyc = row_id // 4, row_id % 4
    left = cx < 2
    b = jnp.where(left, cx, 3 - cx)
    own = b * 2 + cy
    cross = (row_id, (3 - cx) * 2 + cy)
    x_mate = (row_id, (cx + 1 - 2 * (cx % 2)) * 2 + cy)
    y_mate = (row_id, cx * 2 + 1 - cy)
    over_z = [(lax.rem(cz + k, 4) * 4 + cyc, col_id) for k in (1, 2, 3)]
    in_z = [(cz * 4 + lax.rem(cyc + k, 4), col_id) for k in (1, 2, 3)]

    @pl.when(left)
    def _():
        pltpu.make_async_copy(a_hbm.at[:, pl.ds(0, BLOCK)], panel.at[own], load.at[0]).start()

    pltpu.make_async_copy(a_hbm, a, load.at[1]).start()
    barrier = pltpu.get_barrier_semaphore()
    for device in [cross, x_mate, y_mate] + over_z + in_z:
        pl.semaphore_signal(barrier, inc=1, device_id=device, device_id_type=MESH)
    pl.semaphore_wait(barrier, 9)

    @pl.when(left)
    def _():
        pltpu.make_async_copy(a_hbm.at[:, pl.ds(0, BLOCK)], panel.at[own], load.at[0]).wait()

    def piece(j, c):
        return panel.at[j, pl.ds(c * CR, CR), :]

    def send(j, c, sent, got, device):
        return pltpu.make_async_remote_copy(
            piece(j, c), piece(j, c), sent, got, device_id=device, device_id_type=MESH
        )

    flip_x, flip_y = (1 - b) * 2 + cy, b * 2 + 1 - cy
    flip_both = (1 - b) * 2 + 1 - cy

    def plan(c):
        if c % 2 == 0:
            return x_mate, flip_x, y_mate, flip_y
        return y_mate, flip_y, x_mate, flip_x

    def start0(c):
        @pl.when(left)
        def _():
            send(own, c, sent0.at[c], got0.at[c], cross).start()

    def start1(c):
        @pl.when(jnp.logical_not(left))
        def _():
            send(own, c, sent0.at[c], got0.at[c], cross).wait_recv()

        send(own, c, sent1.at[c], got1.at[c], plan(c)[0]).start()

    def start2(c):
        mate1, j1, mate2, _ = plan(c)
        send(j1, c, sent1.at[c], got1.at[c], mate1).wait_recv()
        send(own, c, sent2.at[c, 0], got2.at[c, 0], mate2).start()
        send(j1, c, sent2.at[c, 1], got2.at[c, 1], mate2).start()

    def finish2(c):
        _, _, mate2, j2 = plan(c)
        send(j2, c, sent2.at[c, 0], got2.at[c, 0], mate2).wait_recv()
        send(flip_both, c, sent2.at[c, 1], got2.at[c, 1], mate2).wait_recv()

    ahead0, ahead1 = 6, 3

    def tick(t):
        if t + ahead0 < NC:
            start0(t + ahead0)
        if t + ahead1 < NC:
            start1(t + ahead1)
        if t < NC:
            start2(t)

    for c in range(ahead0):
        start0(c)
    for c in range(ahead1):
        start1(c)

    head = panel.at[:, pl.ds(0, BLOCK), :]
    a_owner = cyc == col_id % 4
    first_z = col_id // 4

    def head_local(slot):
        return pltpu.make_async_copy(head, heads.at[slot], head_got.at[slot])

    def head_copy(source, slot, k, base, device):
        return pltpu.make_async_remote_copy(
            source, heads.at[slot], head_sent.at[base + k], head_got.at[slot],
            device_id=device, device_id_type=MESH,
        )

    sources = [(cz == 0, cyc, 0), (a_owner & (cz == first_z), 4, 3), (a_owner & (cz == first_z + 2), 5, 6)]

    def head_out():
        for mine, slot, base in sources:

            @pl.when(mine)
            def _(slot=slot, base=base):
                head_local(slot).start()
                for k in range(3):
                    head_copy(head, slot, k, base, over_z[k]).start()

    def head_spread():
        head_local(cyc).wait()
        for k in range(3):
            head_copy(heads.at[cyc], cyc, k, 9, in_z[k]).start()

        @pl.when(a_owner)
        def _():
            for slot, base in ((4, 12), (5, 15)):
                head_local(slot).wait()
                for k in range(3):
                    head_copy(heads.at[slot], slot, k, base, in_z[k]).start()

    def head_in():
        for k in (1, 2, 3):
            head_local(lax.rem(cyc + k, 4)).wait()

        @pl.when(jnp.logical_not(a_owner))
        def _():
            for slot in (4, 5):
                head_local(slot).wait()

    def head_done():
        for mine, slot, base in sources:

            @pl.when(mine)
            def _(slot=slot, base=base):
                for k in range(3):
                    head_copy(head, slot, k, base, over_z[k]).wait_send()

        for k in range(3):
            head_copy(heads.at[cyc], cyc, k, 9, in_z[k]).wait_send()

        @pl.when(a_owner)
        def _():
            for slot, base in ((4, 12), (5, 15)):
                for k in range(3):
                    head_copy(heads.at[slot], slot, k, base, in_z[k]).wait_send()

    t = 0

    def advance():
        nonlocal t
        tick(t)
        t += 1

    advance()
    advance()
    finish2(0)
    head_out()
    advance()
    advance()
    head_spread()
    advance()
    advance()
    head_in()

    lower = iota((BLOCK, BLOCK), 0) >= iota((BLOCK, BLOCK), 1)
    for i in range(4):
        rows = slice(i * BLOCK, (i + 1) * BLOCK)
        for j in range(i):
            block = heads[i, j]
            work[rows, j * BLOCK : (j + 1) * BLOCK] = block
            work[j * BLOCK : (j + 1) * BLOCK, rows] = jnp.transpose(block)
        block = heads[i, i]
        work[rows, rows] = jnp.where(lower, block, jnp.transpose(block))
        for j in range(4):
            unit = jnp.where(iota((BLOCK, BLOCK), 0) == iota((BLOCK, BLOCK), 1), float(i == j), 0.0)
            work[rows, PANEL + j * BLOCK : PANEL + (j + 1) * BLOCK] = unit
            factor_t[rows, j * BLOCK : (j + 1) * BLOCK] = jnp.zeros((BLOCK, BLOCK), F32)

    for k in range(4):
        rows = slice(k * BLOCK, (k + 1) * BLOCK)
        carry = [work[k * BLOCK + g * 8 : k * BLOCK + g * 8 + 8, rows] for g in range(16)]
        carry += [
            work[k * BLOCK + g * 8 : k * BLOCK + g * 8 + 8, PANEL + k * BLOCK : PANEL + (k + 1) * BLOCK]
            for g in range(16)
        ]
        carry = tuple(carry)
        for part in range(4):
            carry = lax.fori_loop(
                part * 4, part * 4 + 4, lambda g, v: eliminate(g, v, diag_f, diag_x), carry
            )
            if part % 2:
                advance()
        factor_t[rows, rows] = diag_f[...]
        right = (k + 1) * BLOCK
        width = PANEL + (k + 1) * BLOCK - right
        solved = jnp.dot(diag_x[...], work[rows, right : right + width], precision=HIGHEST)
        work[rows, right : right + width] = solved
        count = PANEL - right
        if count:
            factor_t[rows, right:PANEL] = solved[:, :count]
            turned = jnp.transpose(solved[:, :count])
            work[right:PANEL, right : right + width] -= jnp.dot(turned, solved, precision=HIGHEST)
        advance()

    columns = jnp.concatenate(
        [jnp.concatenate([heads[4 + i, j] for j in range(4)], axis=1) for i in range(2)], axis=0
    )
    solved = lax.dot_general(
        work[:, PANEL:], columns, (((1,), (1,)), ((), ())), precision=HIGHEST, preferred_element_type=F32
    )
    turned = jnp.transpose(work[:, PANEL:])
    weight = jnp.dot(turned, solved, precision=HIGHEST)
    work[:, :PANEL] = turned
    own_panel = col_id < PANEL // BLOCK
    direct = -work[:, pl.ds(pl.multiple_of(jnp.minimum(col_id, 3) * BLOCK, BLOCK), BLOCK)]
    weight = jnp.concatenate([jnp.where(own_panel, direct, weight[:, :BLOCK]), weight[:, BLOCK:]], axis=1)
    high = weight.astype(BF16)
    w_high[...] = high
    w_low[...] = (weight - high.astype(F32)).astype(BF16)
    while t < NC:
        advance()

    pltpu.make_async_copy(a_hbm, a, load.at[1]).wait()
    in_panel = iota((CR, CH), 1) < jnp.where(own_panel, BLOCK, 0)
    dot = functools.partial(jnp.dot, preferred_element_type=F32)
    for c in range(NC):
        if c:
            finish2(c)
        at = slice(c * CR, (c + 1) * CR)
        left_rows = jnp.concatenate([panel[j, at, :] for j in range(4)], axis=1)
        high = left_rows.astype(BF16)
        low = (left_rows - high.astype(F32)).astype(BF16)
        update = dot(high, w_high[...]) + (dot(high, w_low[...]) + dot(low, w_high[...]))
        out[at, :] = jnp.where(in_panel, 0.0, a[at, :]) - update
        if c == 0:

            @pl.when(row_id < PANEL // BLOCK)
            def _():
                d, j = jnp.minimum(row_id, 3), jnp.minimum(col_id, 3)
                block = factor_t[
                    pl.ds(pl.multiple_of(j * BLOCK, BLOCK), BLOCK), pl.ds(pl.multiple_of(d * BLOCK, BLOCK), BLOCK)
                ]
                out[:BLOCK, :BLOCK] = jnp.where(own_panel, jnp.transpose(block), a[:BLOCK, :BLOCK])
                out[:BLOCK, BLOCK:] = a[:BLOCK, BLOCK:]

    for c in range(NC):

        @pl.when(left)
        def _(c=c):
            send(own, c, sent0.at[c], got0.at[c], cross).wait_send()

        mate1, j1, mate2, _ = plan(c)
        send(own, c, sent1.at[c], got1.at[c], mate1).wait_send()
        send(own, c, sent2.at[c, 0], got2.at[c, 0], mate2).wait_send()
        send(j1, c, sent2.at[c, 1], got2.at[c, 1], mate2).wait_send()
    head_done()


def panel_step(combined):
    dma = pltpu.SemaphoreType.DMA
    return pl.pallas_call(
        panel_kernel,
        out_shape=jax.ShapeDtypeStruct((RH, CH), F32),
        in_specs=[pl.BlockSpec(memory_space=pl.ANY)],
        out_specs=pl.BlockSpec(memory_space=pltpu.VMEM),
        scratch_shapes=[
            pltpu.VMEM((RH, CH), F32),
            pltpu.VMEM((4, RH, BLOCK), F32),
            pltpu.VMEM((6, 4, BLOCK, BLOCK), F32),
            pltpu.VMEM((PANEL, 2 * PANEL), F32),
            pltpu.VMEM((PANEL, PANEL), F32),
            pltpu.VMEM((PANEL, CH), BF16),
            pltpu.VMEM((PANEL, CH), BF16),
            pltpu.VMEM((BLOCK, BLOCK), F32),
            pltpu.VMEM((BLOCK, BLOCK), F32),
            dma((2,)),
            dma((NC,)),
            dma((NC,)),
            dma((NC,)),
            dma((NC,)),
            dma((NC, 2)),
            dma((NC, 2)),
            dma((18,)),
            dma((6,)),
        ],
        compiler_params=pltpu.CompilerParams(
            collective_id=0, has_side_effects=True, vmem_limit_bytes=VMEM_LIMIT
        ),
        name="panel_step",
    )(combined)


def shards(grace_slab, goce_slab, grace_weight, goce_weight, kaula_prior, row_target, column_target):
    row_id, col_id = lax.axis_index("prow"), lax.axis_index("pcol")
    targets = lax.dynamic_slice_in_dim(row_target, row_id * RH, RH)
    targets, order = lax.sort((targets, jnp.arange(RH, dtype=jnp.int32)), num_keys=1)
    local = targets.reshape(NPR, 1, GR) - jnp.arange(NPR, dtype=jnp.int32)[:, None, None] * RH
    places = jnp.pad(linear(local), ((0, 0), (0, 0), (0, PLACES - GR)))
    col_targets = lax.dynamic_slice_in_dim(column_target, col_id * CH, CH)
    split_rows = grace_slab.reshape(RH // 8, 8, 2, 128).transpose(0, 2, 1, 3).reshape(2 * RH, 128)
    rows, places = exchange(linear(order), col_targets, column_target, places, split_rows)
    weights = jnp.concatenate([grace_weight, goce_weight])
    combined = place_rows(places.reshape(-1), weights, kaula_prior, rows, goce_slab)
    return panel_step(combined)


def solution(mesh):
    return jax.shard_map(
        shards,
        mesh=mesh,
        in_specs=(P("prow", "pcol"), P("prow", "pcol"), P(), P(), P("pcol"), P(), P()),
        out_specs=P("prow", "pcol"),
        check_vma=False,
    )
```

```python
import functools

import jax
import jax.numpy as jnp
from jax import lax
from jax.experimental import pallas as pl
from jax.experimental.pallas import tpu as pltpu
from jax.sharding import PartitionSpec as P

F32, BF16 = jnp.float32, jnp.bfloat16
MESH = pl.DeviceIdType.MESH
HIGHEST = lax.Precision.HIGHEST
PANEL, BLOCK = 512, 128
NPR, NPC = 16, 8
RH, CH = 5632, 256
GR, GC = RH // NPR, CH // NPC
QR = GR // 4
PIECES = [(0, BLOCK)] + [(at, 256) for at in range(BLOCK, RH - 256, 256)] + [(RH - BLOCK, BLOCK)]
NC = len(PIECES)
VMEM_LIMIT = 60 * 2**20


def iota(shape, dim):
    return lax.broadcasted_iota(jnp.int32, shape, dim)


def select_columns(values, onehot):
    high = values.astype(BF16)
    rest = values - high.astype(F32)
    middle = rest.astype(BF16)
    low = (rest - middle.astype(F32)).astype(BF16)
    dot = functools.partial(jnp.dot, preferred_element_type=F32)
    return dot(high, onehot) + dot(middle, onehot) + dot(low, onehot)


def regroup(parts, lane):
    results = []
    for m in range(4):
        joined = None
        for k in range(4):
            moved = parts[k] if k == m else pltpu.roll(parts[k], ((k - m) * GC) % 128, 1)
            joined = moved if k == 0 else jnp.where(lane // GC == k, moved, joined)
        results.append(joined)
    return results


def linear(row):
    return row // 8 * 16 + row % 8


def turn_row(row_id, col_id, step):
    return jnp.bitwise_xor(row_id, lax.rem(step + 2 * col_id, NPR))


def turn_col(row_id, col_id, k):
    return jnp.bitwise_xor(col_id, lax.rem(k + row_id, NPC))


def exchange_kernel(
    order, col_all, places, x, out, places_out,
    rows, packed, received, pick_out, pick_in, sent, got, place_sent, place_got,
):
    row_id, col_id = lax.axis_index("prow"), lax.axis_index("pcol")
    me = row_id * NPC + col_id
    lane = iota((QR, 128), 1)

    barrier = pltpu.get_barrier_semaphore()

    def greet(k, carry):
        to = lax.rem(me + k, NPR * NPC)
        pl.semaphore_signal(barrier, inc=1, device_id=(to // NPC, to % NPC), device_id_type=MESH)
        return carry

    lax.fori_loop(1, NPR * NPC, greet, 0)

    mine = [col_all[pl.ds(col_id * 2 + h, 1), :].astype(F32) for h in range(2)]
    across = jnp.concatenate(mine, axis=1)
    down = jnp.concatenate([jnp.transpose(jnp.broadcast_to(v, (128, 128))) for v in mine], axis=0)
    below = (jnp.concatenate([down, down], axis=1) > across).astype(F32)
    rank = jnp.sum(below, axis=1, keepdims=True).astype(jnp.int32)
    pick_out[...] = jnp.where(rank == iota((CH, CH), 1), 1.0, 0.0).astype(BF16)

    def pack(step):
        dest = turn_row(row_id, col_id, step)
        base = dest * GR

        def gather(i, carry):
            for u in range(16):
                at = order[base + i * 16 + u]
                tile, sub = i * 2 + u // 8, u % 8
                rows[tile, 0, sub : sub + 1, :] = x[pl.ds(at, 1), :]
                rows[tile, 1, sub : sub + 1, :] = x[pl.ds(at + 8, 1), :]
            return carry

        lax.fori_loop(0, GR // 16, gather, 0)
        taken = jnp.concatenate([rows[:, h].reshape(GR, 128) for h in range(2)], axis=1)
        picked = select_columns(taken, pick_out[...])
        for half in range(2):
            parts = [picked[g * QR : (g + 1) * QR, half * 128 : half * 128 + 128] for g in range(4)]
            for q, joined in enumerate(regroup(parts, lane)):
                packed[dest * NPC + half * 4 + q] = joined

    def chunk_copy(row, col):
        other = row * NPC + col
        return pltpu.make_async_remote_copy(
            packed.at[other], received.at[me], sent.at[other], got.at[me],
            device_id=(row, col), device_id_type=MESH,
        )

    def chunk_from(row, col):
        other = row * NPC + col
        return pltpu.make_async_remote_copy(
            packed.at[other], received.at[other], sent.at[other], got.at[other],
            device_id=(row, col), device_id_type=MESH,
        )

    def place_copy(row, slot):
        return pltpu.make_async_remote_copy(
            places.at[row], places_out.at[slot], place_sent.at[row], place_got.at[slot],
            device_id=(row, col_id), device_id_type=MESH,
        )

    def own_copy():
        return pltpu.make_async_copy(packed.at[me], received.at[me], got.at[me])

    def own_places():
        return pltpu.make_async_copy(places.at[row_id], places_out.at[row_id], place_got.at[row_id])

    def each(step, remote, local):
        row = turn_row(row_id, col_id, step)
        for k in range(NPC):
            col = turn_col(row_id, col_id, k)
            inside = (row == row_id) & (col == col_id)

            @pl.when(jnp.logical_not(inside))
            def _(col=col):
                remote(row, col)

            if local is not None:
                pl.when(inside)(local)

    pack(0)
    pl.semaphore_wait(barrier, NPR * NPC - 1)

    def forward(step, carry):
        @pl.when(step < NPR - 1)
        def _():
            pack(step + 1)

        row = turn_row(row_id, col_id, step)

        @pl.when(row != row_id)
        def _():
            place_copy(row, row_id).start()

        @pl.when(row == row_id)
        def _():
            own_places().start()

        each(step, lambda r, c: chunk_copy(r, c).start(), lambda: own_copy().start())
        return carry

    lax.fori_loop(0, NPR, forward, 0)

    source = jnp.zeros((CH, 128), F32)
    here = col_id * CH + iota((CH, 128), 0)
    for r in range(16):
        source += jnp.where(col_all[r : r + 1, :] == here, float(r // 2), 0.0)
    source = jnp.sum(source, axis=1, keepdims=True)
    across = jnp.transpose(jnp.broadcast_to(source, (CH, 128)))[0:1, :]
    earlier = (source == across) & (iota((CH, CH), 0) < iota((CH, CH), 1))
    rank = jnp.sum(jnp.where(earlier, 1.0, 0.0), axis=0, keepdims=True)
    arrival = (across * GC + rank).astype(jnp.int32)
    pick_in[...] = jnp.where(iota((CH, CH), 0) == arrival, 1.0, 0.0).astype(BF16)

    def arrive(step, carry):
        origin = turn_row(row_id, col_id, step)

        @pl.when(origin != row_id)
        def _():
            place_copy(origin, origin).wait_recv()

        @pl.when(origin == row_id)
        def _():
            own_places().wait()

        each(step, lambda r, c: chunk_from(r, c).wait_recv(), lambda: own_copy().wait())
        halves = [regroup([received[origin * NPC + h * 4 + q] for q in range(4)], lane) for h in range(2)]
        joined = jnp.concatenate(
            [jnp.concatenate([halves[0][g], halves[1][g]], axis=1) for g in range(4)], axis=0
        )
        picked = select_columns(joined, pick_in[...])
        for h in range(2):
            out[origin, :, h] = picked[:, h * 128 : h * 128 + 128].reshape(GR // 8, 8, 128)
        return carry

    lax.fori_loop(0, NPR, arrive, 0)

    def leave(step, carry):
        row = turn_row(row_id, col_id, step)

        @pl.when(row != row_id)
        def _():
            place_copy(row, row_id).wait_send()

        each(step, lambda r, c: chunk_copy(r, c).wait_send(), None)
        return carry

    lax.fori_loop(0, NPR, leave, 0)


def exchange(order, col_all, places, x):
    dma, vmem = pltpu.SemaphoreType.DMA, pl.BlockSpec(memory_space=pltpu.VMEM)
    return pl.pallas_call(
        exchange_kernel,
        out_shape=(
            jax.ShapeDtypeStruct((NPR, GR // 8, 2, 8, 128), F32),
            jax.ShapeDtypeStruct((NPR, 1, GR), jnp.int32),
        ),
        in_specs=[pl.BlockSpec(memory_space=pltpu.SMEM)] + [vmem] * 3,
        out_specs=(vmem, vmem),
        scratch_shapes=[
            pltpu.VMEM((GR // 8, 2, 8, 128), F32),
            pltpu.VMEM((NPR * NPC, QR, 128), F32),
            pltpu.VMEM((NPR * NPC, QR, 128), F32),
            pltpu.VMEM((CH, CH), BF16),
            pltpu.VMEM((CH, CH), BF16),
            dma((NPR * NPC,)),
            dma((NPR * NPC,)),
            dma((NPR,)),
            dma((NPR,)),
        ],
        compiler_params=pltpu.CompilerParams(
            collective_id=1, has_side_effects=True, vmem_limit_bytes=VMEM_LIMIT
        ),
        name="exchange",
    )(order, col_all.reshape(16, 128), places, x)


STEPS = 4
STEP_PARTS, OUT_ROWS = NPR // STEPS, RH // STEPS


def place_kernel(place, weight_a, weight_b, kaula, rows, goce, out, moved):
    step = pl.program_id(0)
    row_id, col_id = lax.axis_index("prow"), lax.axis_index("pcol")

    @pl.when(step < STEPS)
    def _():
        for part in range(STEP_PARTS):
            source = step * STEP_PARTS + part

            def scatter(i, carry, part=part, source=source):
                for u in range(16):
                    at = place[source, 0, i * 16 + u]
                    tile, sub = i * 2 + u // 8, u % 8
                    moved[pl.ds(at, 1), :] = rows[part, tile, 0, sub : sub + 1, :]
                    moved[pl.ds(at + 8, 1), :] = rows[part, tile, 1, sub : sub + 1, :]
                return carry

            lax.fori_loop(0, GR // 16, scatter, 0)

    @pl.when(step >= STEPS)
    def _():
        first = pl.multiple_of((step - STEPS) * 2 * OUT_ROWS, 2 * OUT_ROWS)
        block = moved[pl.ds(first, 2 * OUT_ROWS), :].reshape(OUT_ROWS // 8, 2, 8, 128)
        for h in range(2):
            cols = slice(h * 128, h * 128 + 128)
            out[:, cols] = weight_a[0] * block[:, h].reshape(OUT_ROWS, 128) + weight_b[0] * goce[:, cols]

    @pl.when((step == STEPS) & (row_id % NPC == col_id))
    def _():
        equal = iota((BLOCK, BLOCK), 0) == iota((BLOCK, BLOCK), 1)
        for half in range(2):
            cols = slice(half * BLOCK, (half + 1) * BLOCK)
            add = jnp.where(equal & (row_id // NPC == half), kaula[:, cols], 0.0)
            out[:BLOCK, cols] = out[:BLOCK, cols] + add


def place_rows(place, weight_a, weight_b, kaula, rows, goce):
    smem = pl.BlockSpec(memory_space=pltpu.SMEM)
    return pl.pallas_call(
        place_kernel,
        out_shape=jax.ShapeDtypeStruct((RH, CH), F32),
        grid=(2 * STEPS,),
        in_specs=[
            smem,
            smem,
            smem,
            pl.BlockSpec((1, CH), lambda i: (0, 0)),
            pl.BlockSpec(
                (STEP_PARTS, GR // 8, 2, 8, 128), lambda i: (jnp.minimum(i, STEPS - 1), 0, 0, 0, 0)
            ),
            pl.BlockSpec((OUT_ROWS, CH), lambda i: (jnp.maximum(i - STEPS, 0), 0)),
        ],
        out_specs=pl.BlockSpec((OUT_ROWS, CH), lambda i: (jnp.maximum(i - STEPS, 0), 0)),
        scratch_shapes=[pltpu.VMEM((2 * RH, 128), F32)],
        compiler_params=pltpu.CompilerParams(vmem_limit_bytes=VMEM_LIMIT),
        name="place_rows",
    )(place, weight_a, weight_b, kaula.reshape(1, CH), rows, goce)


def across_rows(v, s):
    return jnp.broadcast_to(v[s : s + 1, :], (8, 128))


def across_lanes(v, t):
    return jnp.broadcast_to(v[:, t : t + 1], (8, 128))


def eliminate(group, carry, n, factor_t, inverse):
    d, x = list(carry[:n]), list(carry[n:])
    lane, sub = iota((8, 128), 1), iota((8, 128), 0)
    f_rows, x_rows = jnp.zeros((8, 128), F32), jnp.zeros((8, 128), F32)
    pivots = jnp.ones((8, 128), F32)
    z, zx = d[0], x[0]
    own = [across_lanes(z, t) for t in range(8)]
    for s in range(8):
        here = sub == s
        pivot, row, x_row = across_rows(own[s], s), across_rows(z, s), across_rows(zx, s)
        r = pltpu.reciprocal(pivot, approx=True)
        r = r * (2.0 - pivot * r)
        r = r * (2.0 - pivot * r)
        f_rows, x_rows = jnp.where(here, row, f_rows), jnp.where(here, x_row, x_rows)
        pivots = jnp.where(here, pivot, pivots)
        c = own[s] * r
        z = jnp.where(here, row * r, z - c * row)
        zx = jnp.where(here, x_row * r, zx - c * x_row)
        for t in range(s + 1, 8):
            e = across_rows(own[t], s)
            own[t] = jnp.where(here, e * r, own[t] - c * e)
    q = lax.rsqrt(pivots)
    q = q * (1.5 - 0.5 * pivots * q * q)
    at = pl.ds(pl.multiple_of(group * 8, 8), 8)
    live = (lane < 128 - 8 * group) & (lane >= sub)
    factor_t[at, :] = pltpu.roll(jnp.where(live, f_rows * q, 0.0), group * 8, 1)
    inverse[at, :] = x_rows * q
    z_rows, zx_rows = [across_rows(z, t) for t in range(8)], [across_rows(zx, t) for t in range(8)]
    for i in range(1, n):
        di, xi = d[i], x[i]
        for t in range(8):
            c = across_lanes(d[i], t)
            di = di - c * z_rows[t]
            xi = xi - c * zx_rows[t]
        d[i], x[i] = di, xi
    return tuple([pltpu.roll(v, 120, 1) for v in d[1:] + d[:1]] + x[1:] + x[:1])


def panel_kernel(
    a_hbm, out, a, panel, heads, work, factor_t, w_high, w_low, diag_f, diag_x,
    load, sent0, got0, sent1, got1, sent2, got2, head_sent, head_got,
):
    row_id, col_id = lax.axis_index("prow"), lax.axis_index("pcol")
    cx, cy = col_id // 2, col_id % 2
    cz, cyc = row_id // 4, row_id % 4
    left = cx < 2
    b = jnp.where(left, cx, 3 - cx)
    own = b * 2 + cy
    cross = (row_id, (3 - cx) * 2 + cy)
    x_mate = (row_id, (cx + 1 - 2 * (cx % 2)) * 2 + cy)
    y_mate = (row_id, cx * 2 + 1 - cy)
    over_z = [(lax.rem(cz + k, 4) * 4 + cyc, col_id) for k in (1, 2, 3)]
    core = cyc % 2
    y_near = (cz * 4 + lax.rem(cyc + 2, 4), col_id)
    core_mate = (cz * 4 + cyc + 1 - 2 * core, col_id)

    @pl.when(left)
    def _():
        pltpu.make_async_copy(a_hbm.at[:, pl.ds(0, BLOCK)], panel.at[own], load.at[0]).start()

    pltpu.make_async_copy(a_hbm, a, load.at[1]).start()
    barrier = pltpu.get_barrier_semaphore()
    for device in [cross, x_mate, y_mate, y_near, core_mate] + over_z:
        pl.semaphore_signal(barrier, inc=1, device_id=device, device_id_type=MESH)
    pl.semaphore_wait(barrier, 8)

    @pl.when(left)
    def _():
        pltpu.make_async_copy(a_hbm.at[:, pl.ds(0, BLOCK)], panel.at[own], load.at[0]).wait()

    def piece(j, c):
        return panel.at[j, pl.ds(*PIECES[c]), :]

    def send(j, c, sent, got, device):
        return pltpu.make_async_remote_copy(
            piece(j, c), piece(j, c), sent, got, device_id=device, device_id_type=MESH
        )

    flip_x, flip_y = (1 - b) * 2 + cy, b * 2 + 1 - cy
    flip_both = (1 - b) * 2 + 1 - cy

    def plan(c):
        if c % 2 == 0:
            return x_mate, flip_x, y_mate, flip_y
        return y_mate, flip_y, x_mate, flip_x

    def start0(c):
        @pl.when(left)
        def _():
            send(own, c, sent0.at[c], got0.at[c], cross).start()

    def start1(c):
        @pl.when(jnp.logical_not(left))
        def _():
            send(own, c, sent0.at[c], got0.at[c], cross).wait_recv()

        send(own, c, sent1.at[c], got1.at[c], plan(c)[0]).start()

    def start2(c):
        mate1, j1, mate2, _ = plan(c)
        send(j1, c, sent1.at[c], got1.at[c], mate1).wait_recv()
        send(own, c, sent2.at[c, 0], got2.at[c, 0], mate2).start()
        send(j1, c, sent2.at[c, 1], got2.at[c, 1], mate2).start()

    def finish2(c):
        _, _, mate2, j2 = plan(c)
        send(j2, c, sent2.at[c, 0], got2.at[c, 0], mate2).wait_recv()
        send(flip_both, c, sent2.at[c, 1], got2.at[c, 1], mate2).wait_recv()

    head = panel.at[:, pl.ds(0, BLOCK), :]
    a_owner = cyc == col_id % 4
    a_core = core == col_id % 2
    first_z = col_id // 4
    far = lax.rem(cyc + 2, 4)

    def head_local(slot):
        return pltpu.make_async_copy(head, heads.at[slot], head_got.at[slot])

    def head_copy(source, slot, k, device):
        return pltpu.make_async_remote_copy(
            source, heads.at[slot], head_sent.at[k], head_got.at[slot],
            device_id=device, device_id_type=MESH,
        )

    sources = [(cz == 0, cyc, 0), (a_owner & (cz == first_z), 4, 3), (a_owner & (cz == first_z + 2), 5, 6)]

    def head_z():
        for mine, slot, base in sources:

            @pl.when(mine)
            def _(slot=slot, base=base):
                head_local(slot).start()
                for k in range(3):
                    head_copy(head, slot, base + k, over_z[k]).start()

    def to_y(slot, k):
        return head_copy(heads.at[slot], slot, k, y_near)

    def to_core(slot, k):
        return head_copy(heads.at[slot], slot, k, core_mate)

    def head_y():
        head_local(cyc).wait()
        to_y(cyc, 9).start()

        @pl.when(a_owner)
        def _():
            for k, slot in enumerate((4, 5)):
                head_local(slot).wait()
                to_y(slot, 10 + k).start()

    def head_core():
        head_local(far).wait()
        to_core(cyc, 12).start()
        to_core(far, 13).start()

        @pl.when(a_core)
        def _():
            for k, slot in enumerate((4, 5)):

                @pl.when(jnp.logical_not(a_owner))
                def _(slot=slot):
                    head_local(slot).wait()

                to_core(slot, 14 + k).start()

    def head_in():
        head_local(cyc + 1 - 2 * core).wait()
        head_local(lax.rem(cyc + 3 - 2 * core, 4)).wait()

        @pl.when(jnp.logical_not(a_core))
        def _():
            for slot in (4, 5):
                head_local(slot).wait()

    def head_done():
        for mine, slot, base in sources:

            @pl.when(mine)
            def _(slot=slot, base=base):
                for k in range(3):
                    head_copy(head, slot, base + k, over_z[k]).wait_send()

        to_y(cyc, 9).wait_send()
        to_core(cyc, 12).wait_send()
        to_core(far, 13).wait_send()
        for k, slot in enumerate((4, 5)):

            @pl.when(a_owner)
            def _(k=k, slot=slot):
                to_y(slot, 10 + k).wait_send()

            @pl.when(a_core)
            def _(k=k, slot=slot):
                to_core(slot, 14 + k).wait_send()

    next0, next1, next2 = 6, 3, 2

    def advance():
        nonlocal next0, next1, next2
        if next0 < NC:
            start0(next0)
        if next1 < NC:
            start1(next1)
        if next2 < NC:
            start2(next2)
        next0, next1, next2 = next0 + 1, next1 + 1, next2 + 1

    for c in range(next0):
        start0(c)
    start1(0)
    start2(0)
    start1(1)
    finish2(0)
    head_z()
    start1(2)
    start2(1)
    advance()
    head_y()
    advance()
    head_core()
    advance()
    head_in()

    lower = iota((BLOCK, BLOCK), 0) >= iota((BLOCK, BLOCK), 1)
    for i in range(4):
        rows = slice(i * BLOCK, (i + 1) * BLOCK)
        for j in range(i):
            block = heads[i, j]
            work[rows, j * BLOCK : (j + 1) * BLOCK] = block
            work[j * BLOCK : (j + 1) * BLOCK, rows] = jnp.transpose(block)
        block = heads[i, i]
        work[rows, rows] = jnp.where(lower, block, jnp.transpose(block))
        for j in range(4):
            unit = jnp.where(iota((BLOCK, BLOCK), 0) == iota((BLOCK, BLOCK), 1), float(i == j), 0.0)
            work[rows, PANEL + j * BLOCK : PANEL + (j + 1) * BLOCK] = unit
            factor_t[rows, j * BLOCK : (j + 1) * BLOCK] = jnp.zeros((BLOCK, BLOCK), F32)

    for k in range(4):
        rows = slice(k * BLOCK, (k + 1) * BLOCK)
        carry = [work[k * BLOCK + g * 8 : k * BLOCK + g * 8 + 8, rows] for g in range(16)]
        carry += [
            work[k * BLOCK + g * 8 : k * BLOCK + g * 8 + 8, PANEL + k * BLOCK : PANEL + (k + 1) * BLOCK]
            for g in range(16)
        ]
        d, x = carry[:16], carry[16:]
        for part in range(4):
            n = 16 - 4 * part
            carry = lax.fori_loop(
                part * 4, part * 4 + 4, lambda g, v, n=n: eliminate(g, v, n, diag_f, diag_x), tuple(d + x)
            )
            d, x = list(carry[: n - 4]), list(carry[n : 2 * n - 4])
            if part in (0, 2):
                advance()
        factor_t[rows, rows] = diag_f[...]
        right = (k + 1) * BLOCK
        width = PANEL + (k + 1) * BLOCK - right
        solved = jnp.dot(diag_x[...], work[rows, right : right + width], precision=HIGHEST)
        work[rows, right : right + width] = solved
        count = PANEL - right
        if count:
            factor_t[rows, right:PANEL] = solved[:, :count]
            turned = jnp.transpose(solved[:, :count])
            work[right:PANEL, right : right + width] -= jnp.dot(turned, solved, precision=HIGHEST)

    columns = jnp.concatenate(
        [jnp.concatenate([heads[4 + i, j] for j in range(4)], axis=1) for i in range(2)], axis=0
    )
    solved = lax.dot_general(
        work[:, PANEL:], columns, (((1,), (1,)), ((), ())), precision=HIGHEST, preferred_element_type=F32
    )
    turned = jnp.transpose(work[:, PANEL:])
    weight = jnp.dot(turned, solved, precision=HIGHEST)
    work[:, :PANEL] = turned
    own_panel = col_id < PANEL // BLOCK
    direct = -work[:, pl.ds(pl.multiple_of(jnp.minimum(col_id, 3) * BLOCK, BLOCK), BLOCK)]
    weight = jnp.concatenate([jnp.where(own_panel, direct, weight[:, :BLOCK]), weight[:, BLOCK:]], axis=1)
    high = weight.astype(BF16)
    w_high[...] = high
    w_low[...] = (weight - high.astype(F32)).astype(BF16)
    pltpu.make_async_copy(a_hbm, a, load.at[1]).wait()
    dot = functools.partial(jnp.dot, preferred_element_type=F32)

    def update(c):
        if c:
            finish2(c)
        start, size = PIECES[c]
        at = slice(start, start + size)
        in_panel = iota((size, CH), 1) < jnp.where(own_panel, BLOCK, 0)
        left_rows = jnp.concatenate([panel[j, at, :] for j in range(4)], axis=1)
        high = left_rows.astype(BF16)
        low = (left_rows - high.astype(F32)).astype(BF16)
        product = dot(high, w_high[...]) + (dot(high, w_low[...]) + dot(low, w_high[...]))
        out[at, :] = jnp.where(in_panel, 0.0, a[at, :]) - product
        if c == 0:

            @pl.when(row_id < PANEL // BLOCK)
            def _():
                d, j = jnp.minimum(row_id, 3), jnp.minimum(col_id, 3)
                block = factor_t[
                    pl.ds(pl.multiple_of(j * BLOCK, BLOCK), BLOCK), pl.ds(pl.multiple_of(d * BLOCK, BLOCK), BLOCK)
                ]
                out[:BLOCK, :BLOCK] = jnp.where(own_panel, jnp.transpose(block), a[:BLOCK, :BLOCK])
                out[:BLOCK, BLOCK:] = a[:BLOCK, BLOCK:]

    done = 0
    while next2 < NC:
        advance()
        for _ in range(2):
            if done <= next2 - 4:
                update(done)
                done += 1
    while done < NC:
        update(done)
        done += 1

    for c in range(NC):

        @pl.when(left)
        def _(c=c):
            send(own, c, sent0.at[c], got0.at[c], cross).wait_send()

        mate1, j1, mate2, _ = plan(c)
        send(own, c, sent1.at[c], got1.at[c], mate1).wait_send()
        send(own, c, sent2.at[c, 0], got2.at[c, 0], mate2).wait_send()
        send(j1, c, sent2.at[c, 1], got2.at[c, 1], mate2).wait_send()
    head_done()


def panel_step(combined):
    dma = pltpu.SemaphoreType.DMA
    return pl.pallas_call(
        panel_kernel,
        out_shape=jax.ShapeDtypeStruct((RH, CH), F32),
        in_specs=[pl.BlockSpec(memory_space=pl.ANY)],
        out_specs=pl.BlockSpec(memory_space=pltpu.VMEM),
        scratch_shapes=[
            pltpu.VMEM((RH, CH), F32),
            pltpu.VMEM((4, RH, BLOCK), F32),
            pltpu.VMEM((6, 4, BLOCK, BLOCK), F32),
            pltpu.VMEM((PANEL, 2 * PANEL), F32),
            pltpu.VMEM((PANEL, PANEL), F32),
            pltpu.VMEM((PANEL, CH), BF16),
            pltpu.VMEM((PANEL, CH), BF16),
            pltpu.VMEM((BLOCK, BLOCK), F32),
            pltpu.VMEM((BLOCK, BLOCK), F32),
            dma((2,)),
            dma((NC,)),
            dma((NC,)),
            dma((NC,)),
            dma((NC,)),
            dma((NC, 2)),
            dma((NC, 2)),
            dma((16,)),
            dma((6,)),
        ],
        compiler_params=pltpu.CompilerParams(
            collective_id=0, has_side_effects=True, vmem_limit_bytes=VMEM_LIMIT
        ),
        name="panel_step",
    )(combined)


def shards(grace_slab, goce_slab, grace_weight, goce_weight, kaula_prior, row_target, column_target):
    row_id = lax.axis_index("prow")
    targets = lax.dynamic_slice_in_dim(row_target, row_id * RH, RH)
    targets, order = lax.sort((targets, jnp.arange(RH, dtype=jnp.int32)), num_keys=1)
    places = linear(targets.reshape(NPR, 1, GR) - jnp.arange(NPR, dtype=jnp.int32)[:, None, None] * RH)
    split_rows = grace_slab.reshape(RH // 8, 8, 2, 128).transpose(0, 2, 1, 3).reshape(2 * RH, 128)
    rows, places = exchange(linear(order), column_target, places, split_rows)
    combined = place_rows(places, grace_weight, goce_weight, kaula_prior, rows, goce_slab)
    return panel_step(combined)


def solution(mesh):
    return jax.shard_map(
        shards,
        mesh=mesh,
        in_specs=(P("prow", "pcol"), P("prow", "pcol"), P(), P(), P("pcol"), P(), P()),
        out_specs=P("prow", "pcol"),
        check_vma=False,
    )
```

```python
import functools

import jax
import jax.numpy as jnp
from jax import lax
from jax.experimental import pallas as pl
from jax.experimental.pallas import tpu as pltpu
from jax.sharding import PartitionSpec as P

F32, BF16 = jnp.float32, jnp.bfloat16
MESH = pl.DeviceIdType.MESH
HIGHEST = lax.Precision.HIGHEST
PANEL, BLOCK = 512, 128
NPR, NPC = 16, 8
RH, CH = 5632, 256
GR, GC = RH // NPR, CH // NPC
QR = GR // 4
PIECES = [(0, BLOCK)] + [(at, 256) for at in range(BLOCK, RH - 256, 256)] + [(RH - BLOCK, BLOCK)]
NC = len(PIECES)
VMEM_LIMIT = 60 * 2**20
INV_ROWS = 48


def iota(shape, dim):
    return lax.broadcasted_iota(jnp.int32, shape, dim)


def select_columns(values, onehot):
    high = values.astype(BF16)
    rest = values - high.astype(F32)
    middle = rest.astype(BF16)
    low = (rest - middle.astype(F32)).astype(BF16)
    dot = functools.partial(jnp.dot, preferred_element_type=F32)
    return dot(high, onehot) + dot(middle, onehot) + dot(low, onehot)


def regroup(parts, lane):
    results = []
    for m in range(4):
        joined = None
        for k in range(4):
            moved = parts[k] if k == m else pltpu.roll(parts[k], ((k - m) * GC) % 128, 1)
            joined = moved if k == 0 else jnp.where(lane // GC == k, moved, joined)
        results.append(joined)
    return results


def linear(row):
    return row // 8 * 16 + row % 8


def turn_row(row_id, col_id, step):
    return jnp.bitwise_xor(row_id, lax.rem(step + 2 * col_id, NPR))


def turn_col(row_id, col_id, k):
    return jnp.bitwise_xor(col_id, lax.rem(k + row_id, NPC))


def exchange_kernel(
    order, col_all, places, x, out, inverse_out,
    rows, packed, received, places_in, pick_out, pick_in, sent, got, place_sent, place_got,
):
    row_id, col_id = lax.axis_index("prow"), lax.axis_index("pcol")
    me = row_id * NPC + col_id
    lane = iota((QR, 128), 1)

    barrier = pltpu.get_barrier_semaphore()

    def greet(k, carry):
        to = lax.rem(me + k, NPR * NPC)
        pl.semaphore_signal(barrier, inc=1, device_id=(to // NPC, to % NPC), device_id_type=MESH)
        return carry

    lax.fori_loop(1, NPR * NPC, greet, 0)

    mine = [col_all[pl.ds(col_id * 2 + h, 1), :].astype(F32) for h in range(2)]
    across = jnp.concatenate(mine, axis=1)
    down = jnp.concatenate([jnp.transpose(jnp.broadcast_to(v, (128, 128))) for v in mine], axis=0)
    below = (jnp.concatenate([down, down], axis=1) > across).astype(F32)
    rank = jnp.sum(below, axis=1, keepdims=True).astype(jnp.int32)
    pick_out[...] = jnp.where(rank == iota((CH, CH), 1), 1.0, 0.0).astype(BF16)

    def pack(step):
        dest = turn_row(row_id, col_id, step)
        base = dest * GR

        def gather(i, carry):
            for u in range(16):
                at = order[base + i * 16 + u]
                tile, sub = i * 2 + u // 8, u % 8
                rows[tile, 0, sub : sub + 1, :] = x[pl.ds(at, 1), :]
                rows[tile, 1, sub : sub + 1, :] = x[pl.ds(at + 8, 1), :]
            return carry

        lax.fori_loop(0, GR // 16, gather, 0)
        taken = jnp.concatenate([rows[:, h].reshape(GR, 128) for h in range(2)], axis=1)
        picked = select_columns(taken, pick_out[...])
        for half in range(2):
            parts = [picked[g * QR : (g + 1) * QR, half * 128 : half * 128 + 128] for g in range(4)]
            for q, joined in enumerate(regroup(parts, lane)):
                packed[dest * NPC + half * 4 + q] = joined

    def chunk_copy(row, col):
        other = row * NPC + col
        return pltpu.make_async_remote_copy(
            packed.at[other], received.at[me], sent.at[other], got.at[me],
            device_id=(row, col), device_id_type=MESH,
        )

    def chunk_from(row, col):
        other = row * NPC + col
        return pltpu.make_async_remote_copy(
            packed.at[other], received.at[other], sent.at[other], got.at[other],
            device_id=(row, col), device_id_type=MESH,
        )

    def place_copy(row, slot):
        return pltpu.make_async_remote_copy(
            places.at[row], places_in.at[slot], place_sent.at[row], place_got.at[slot],
            device_id=(row, col_id), device_id_type=MESH,
        )

    def own_copy():
        return pltpu.make_async_copy(packed.at[me], received.at[me], got.at[me])

    def own_places():
        return pltpu.make_async_copy(places.at[row_id], places_in.at[row_id], place_got.at[row_id])

    def each(step, remote, local):
        row = turn_row(row_id, col_id, step)
        for k in range(NPC):
            col = turn_col(row_id, col_id, k)
            inside = (row == row_id) & (col == col_id)

            @pl.when(jnp.logical_not(inside))
            def _(col=col):
                remote(row, col)

            if local is not None:
                pl.when(inside)(local)

    pack(0)
    pl.semaphore_wait(barrier, NPR * NPC - 1)
    own_places().start()

    def announce(k, carry):
        place_copy(jnp.bitwise_xor(row_id, k), row_id).start()
        return carry

    lax.fori_loop(1, NPR, announce, 0)

    def forward(step, carry):
        @pl.when(step < NPR - 1)
        def _():
            pack(step + 1)

        each(step, lambda r, c: chunk_copy(r, c).start(), lambda: own_copy().start())
        return carry

    lax.fori_loop(0, NPR, forward, 0)

    source = jnp.zeros((CH, 128), F32)
    here = col_id * CH + iota((CH, 128), 0)
    for r in range(16):
        source += jnp.where(col_all[r : r + 1, :] == here, float(r // 2), 0.0)
    source = jnp.sum(source, axis=1, keepdims=True)
    across = jnp.transpose(jnp.broadcast_to(source, (CH, 128)))[0:1, :]
    earlier = (source == across) & (iota((CH, CH), 0) < iota((CH, CH), 1))
    rank = jnp.sum(jnp.where(earlier, 1.0, 0.0), axis=0, keepdims=True)
    arrival = (across * GC + rank).astype(jnp.int32)
    pick_in[...] = jnp.where(iota((CH, CH), 0) == arrival, 1.0, 0.0).astype(BF16)

    own_places().wait()

    def places_arrive(k, carry):
        origin = jnp.bitwise_xor(row_id, k)
        place_copy(origin, origin).wait_recv()
        return carry

    lax.fori_loop(1, NPR, places_arrive, 0)

    def invert(origin, total):
        place = places_in[origin]
        number = origin * GR + iota((1, GR), 1)
        high, low = number // 64, number % 64
        down = iota((INV_ROWS, GR), 0) == lax.shift_right_logical(place, 7)
        across = jnp.where(iota((BLOCK, GR), 0) == jnp.bitwise_and(place, 127), 1.0, 0.0).astype(BF16)
        for part, scale in ((high, 64.0), (low, 1.0)):
            values = jnp.where(down, part.astype(F32), 0.0).astype(BF16)
            total = total + scale * lax.dot_general(
                values, across, (((1,), (1,)), ((), ())), preferred_element_type=F32
            )
        return total

    number = lax.fori_loop(0, NPR, invert, jnp.zeros((INV_ROWS, BLOCK), F32)).astype(jnp.int32)
    inverse_out[...] = number + lax.shift_right_logical(number, 3) * 8

    def arrive(step, carry):
        origin = turn_row(row_id, col_id, step)
        each(step, lambda r, c: chunk_from(r, c).wait_recv(), lambda: own_copy().wait())
        halves = [regroup([received[origin * NPC + h * 4 + q] for q in range(4)], lane) for h in range(2)]
        joined = jnp.concatenate(
            [jnp.concatenate([halves[0][g], halves[1][g]], axis=1) for g in range(4)], axis=0
        )
        picked = select_columns(joined, pick_in[...])
        for h in range(2):
            out[origin, :, h] = picked[:, h * 128 : h * 128 + 128].reshape(GR // 8, 8, 128)
        return carry

    lax.fori_loop(0, NPR, arrive, 0)

    def leave(step, carry):
        each(step, lambda r, c: chunk_copy(r, c).wait_send(), None)
        return carry

    lax.fori_loop(0, NPR, leave, 0)

    def announced(k, carry):
        place_copy(jnp.bitwise_xor(row_id, k), row_id).wait_send()
        return carry

    lax.fori_loop(1, NPR, announced, 0)


def exchange(order, col_all, places, x):
    dma, vmem = pltpu.SemaphoreType.DMA, pl.BlockSpec(memory_space=pltpu.VMEM)
    return pl.pallas_call(
        exchange_kernel,
        out_shape=(
            jax.ShapeDtypeStruct((NPR, GR // 8, 2, 8, 128), F32),
            jax.ShapeDtypeStruct((INV_ROWS, BLOCK), jnp.int32),
        ),
        in_specs=[pl.BlockSpec(memory_space=pltpu.SMEM)] + [vmem] * 3,
        out_specs=(vmem, vmem),
        scratch_shapes=[
            pltpu.VMEM((GR // 8, 2, 8, 128), F32),
            pltpu.VMEM((NPR * NPC, QR, 128), F32),
            pltpu.VMEM((NPR * NPC, QR, 128), F32),
            pltpu.VMEM((NPR, 1, GR), jnp.int32),
            pltpu.VMEM((CH, CH), BF16),
            pltpu.VMEM((CH, CH), BF16),
            dma((NPR * NPC,)),
            dma((NPR * NPC,)),
            dma((NPR,)),
            dma((NPR,)),
        ],
        compiler_params=pltpu.CompilerParams(
            collective_id=1, has_side_effects=True, vmem_limit_bytes=VMEM_LIMIT
        ),
        name="exchange",
    )(order, col_all.reshape(16, 128), places, x)


def across_rows(v, s):
    return jnp.broadcast_to(v[s : s + 1, :], (8, 128))


def across_lanes(v, t):
    return jnp.broadcast_to(v[:, t : t + 1], (8, 128))


def eliminate(group, carry, n, factor_t, inverse):
    d, x = list(carry[:n]), list(carry[n:])
    lane, sub = iota((8, 128), 1), iota((8, 128), 0)
    f_rows, x_rows = jnp.zeros((8, 128), F32), jnp.zeros((8, 128), F32)
    pivots = jnp.ones((8, 128), F32)
    z, zx = d[0], x[0]
    own = [across_lanes(z, t) for t in range(8)]
    for s in range(8):
        here = sub == s
        pivot, row, x_row = across_rows(own[s], s), across_rows(z, s), across_rows(zx, s)
        r = pltpu.reciprocal(pivot, approx=True)
        r = r * (2.0 - pivot * r)
        r = r * (2.0 - pivot * r)
        f_rows, x_rows = jnp.where(here, row, f_rows), jnp.where(here, x_row, x_rows)
        pivots = jnp.where(here, pivot, pivots)
        c = own[s] * r
        z = jnp.where(here, row * r, z - c * row)
        zx = jnp.where(here, x_row * r, zx - c * x_row)
        for t in range(s + 1, 8):
            e = across_rows(own[t], s)
            own[t] = jnp.where(here, e * r, own[t] - c * e)
    q = lax.rsqrt(pivots)
    q = q * (1.5 - 0.5 * pivots * q * q)
    at = pl.ds(pl.multiple_of(group * 8, 8), 8)
    live = (lane < 128 - 8 * group) & (lane >= sub)
    factor_t[at, :] = pltpu.roll(jnp.where(live, f_rows * q, 0.0), group * 8, 1)
    inverse[at, :] = x_rows * q
    z_rows, zx_rows = [across_rows(z, t) for t in range(8)], [across_rows(zx, t) for t in range(8)]
    for i in range(1, n):
        di, xi = d[i], x[i]
        for t in range(8):
            c = across_lanes(d[i], t)
            di = di - c * z_rows[t]
            xi = xi - c * zx_rows[t]
        d[i], x[i] = di, xi
    return tuple([pltpu.roll(v, 120, 1) for v in d[1:] + d[:1]] + x[1:] + x[:1])


def panel_kernel(
    inverse, weight_a, weight_b, kaula, rows_hbm, goce_hbm, out,
    source, goce, raw, a, panel, heads, work, factor_t, w_high, w_low, diag_f, diag_x,
    load, sent0, got0, sent1, got1, sent2, got2, head_sent, head_got,
):
    row_id, col_id = lax.axis_index("prow"), lax.axis_index("pcol")
    cx, cy = col_id // 2, col_id % 2
    cz, cyc = row_id // 4, row_id % 4
    left = cx < 2
    b = jnp.where(left, cx, 3 - cx)
    own = b * 2 + cy
    cross = (row_id, (3 - cx) * 2 + cy)
    x_mate = (row_id, (cx + 1 - 2 * (cx % 2)) * 2 + cy)
    y_mate = (row_id, cx * 2 + 1 - cy)
    over_z = [(lax.rem(cz + k, 4) * 4 + cyc, col_id) for k in (1, 2, 3)]
    core = cyc % 2
    y_near = (cz * 4 + lax.rem(cyc + 2, 4), col_id)
    core_mate = (cz * 4 + cyc + 1 - 2 * core, col_id)

    fetch = [
        pltpu.make_async_copy(rows_hbm, source, load.at[0]),
        pltpu.make_async_copy(goce_hbm, goce, load.at[1]),
    ]
    for copy in fetch:
        copy.start()
    barrier = pltpu.get_barrier_semaphore()
    for device in [cross, x_mate, y_mate, y_near, core_mate] + over_z:
        pl.semaphore_signal(barrier, inc=1, device_id=device, device_id_type=MESH)

    def build(c):
        start, size = PIECES[c]

        def gather(i, carry):
            for u in range(16):
                at = inverse[start // 128 + i // 8, i % 8 * 16 + u]
                tile, sub = i * 2 + u // 8, u % 8
                raw[tile, 0, sub : sub + 1, :] = source[pl.ds(at, 1), :]
                raw[tile, 1, sub : sub + 1, :] = source[pl.ds(at + 8, 1), :]
            return carry

        lax.fori_loop(0, size // 16, gather, 0)
        at = slice(start, start + size)
        for h in range(2):
            cols = slice(h * BLOCK, (h + 1) * BLOCK)
            moved = raw[: size // 8, h].reshape(size, BLOCK)
            block = weight_a[0] * moved + weight_b[0] * goce[at, cols]
            if c == 0:
                diagonal = iota((BLOCK, BLOCK), 0) == iota((BLOCK, BLOCK), 1)
                here = (row_id % NPC == col_id) & (row_id // NPC == h)
                block = block + jnp.where(diagonal & here, kaula[:, cols], 0.0)
            a[h, at] = block
            if h == 0:

                @pl.when(left)
                def _():
                    panel[own, at] = block

    def piece(j, c):
        return panel.at[j, pl.ds(*PIECES[c]), :]

    def send(j, c, sent, got, device):
        return pltpu.make_async_remote_copy(
            piece(j, c), piece(j, c), sent, got, device_id=device, device_id_type=MESH
        )

    flip_x, flip_y = (1 - b) * 2 + cy, b * 2 + 1 - cy
    flip_both = (1 - b) * 2 + 1 - cy

    def plan(c):
        if c % 2 == 0:
            return x_mate, flip_x, y_mate, flip_y
        return y_mate, flip_y, x_mate, flip_x

    def start0(c):
        @pl.when(left)
        def _():
            send(own, c, sent0.at[c], got0.at[c], cross).start()

    def start1(c):
        @pl.when(jnp.logical_not(left))
        def _():
            send(own, c, sent0.at[c], got0.at[c], cross).wait_recv()

        send(own, c, sent1.at[c], got1.at[c], plan(c)[0]).start()

    def start2(c):
        mate1, j1, mate2, _ = plan(c)
        send(j1, c, sent1.at[c], got1.at[c], mate1).wait_recv()
        send(own, c, sent2.at[c, 0], got2.at[c, 0], mate2).start()
        send(j1, c, sent2.at[c, 1], got2.at[c, 1], mate2).start()

    def finish2(c):
        _, _, mate2, j2 = plan(c)
        send(j2, c, sent2.at[c, 0], got2.at[c, 0], mate2).wait_recv()
        send(flip_both, c, sent2.at[c, 1], got2.at[c, 1], mate2).wait_recv()

    head = panel.at[:, pl.ds(0, BLOCK), :]
    a_owner = cyc == col_id % 4
    a_core = core == col_id % 2
    first_z = col_id // 4
    far = lax.rem(cyc + 2, 4)

    def head_local(slot):
        return pltpu.make_async_copy(head, heads.at[slot], head_got.at[slot])

    def head_copy(source, slot, k, device):
        return pltpu.make_async_remote_copy(
            source, heads.at[slot], head_sent.at[k], head_got.at[slot],
            device_id=device, device_id_type=MESH,
        )

    sources = [(cz == 0, cyc, 0), (a_owner & (cz == first_z), 4, 3), (a_owner & (cz == first_z + 2), 5, 6)]

    def head_z():
        for mine, slot, base in sources:

            @pl.when(mine)
            def _(slot=slot, base=base):
                head_local(slot).start()
                for k in range(3):
                    head_copy(head, slot, base + k, over_z[k]).start()

    def to_y(slot, k):
        return head_copy(heads.at[slot], slot, k, y_near)

    def to_core(slot, k):
        return head_copy(heads.at[slot], slot, k, core_mate)

    def head_y():
        head_local(cyc).wait()
        to_y(cyc, 9).start()

        @pl.when(a_owner)
        def _():
            for k, slot in enumerate((4, 5)):
                head_local(slot).wait()
                to_y(slot, 10 + k).start()

    def head_core():
        head_local(far).wait()
        to_core(cyc, 12).start()
        to_core(far, 13).start()

        @pl.when(a_core)
        def _():
            for k, slot in enumerate((4, 5)):

                @pl.when(jnp.logical_not(a_owner))
                def _(slot=slot):
                    head_local(slot).wait()

                to_core(slot, 14 + k).start()

    def head_in():
        head_local(cyc + 1 - 2 * core).wait()
        head_local(lax.rem(cyc + 3 - 2 * core, 4)).wait()

        @pl.when(jnp.logical_not(a_core))
        def _():
            for slot in (4, 5):
                head_local(slot).wait()

    def head_done():
        for mine, slot, base in sources:

            @pl.when(mine)
            def _(slot=slot, base=base):
                for k in range(3):
                    head_copy(head, slot, base + k, over_z[k]).wait_send()

        to_y(cyc, 9).wait_send()
        to_core(cyc, 12).wait_send()
        to_core(far, 13).wait_send()
        for k, slot in enumerate((4, 5)):

            @pl.when(a_owner)
            def _(k=k, slot=slot):
                to_y(slot, 10 + k).wait_send()

            @pl.when(a_core)
            def _(k=k, slot=slot):
                to_core(slot, 14 + k).wait_send()

    next0, next1, next2 = 6, 3, 2

    def advance():
        nonlocal next0, next1, next2
        if next0 < NC:
            start0(next0)
        if next1 < NC:
            start1(next1)
        if next2 < NC:
            start2(next2)
        if next0 + 1 < NC:
            build(next0 + 1)
        next0, next1, next2 = next0 + 1, next1 + 1, next2 + 1

    for copy in fetch:
        copy.wait()
    build(0)
    pl.semaphore_wait(barrier, 8)
    build(1)
    start0(0)
    build(2)
    start0(1)
    start1(0)
    build(3)
    start0(2)
    start2(0)
    build(4)
    start0(3)
    start1(1)
    finish2(0)
    head_z()
    build(5)
    start0(4)
    start1(2)
    start2(1)
    build(6)
    start0(5)
    advance()
    head_y()
    advance()
    head_core()
    advance()
    head_in()

    lower = iota((BLOCK, BLOCK), 0) >= iota((BLOCK, BLOCK), 1)
    for i in range(4):
        rows = slice(i * BLOCK, (i + 1) * BLOCK)
        for j in range(i):
            block = heads[i, j]
            work[rows, j * BLOCK : (j + 1) * BLOCK] = block
            work[j * BLOCK : (j + 1) * BLOCK, rows] = jnp.transpose(block)
        block = heads[i, i]
        work[rows, rows] = jnp.where(lower, block, jnp.transpose(block))
        for j in range(4):
            unit = jnp.where(iota((BLOCK, BLOCK), 0) == iota((BLOCK, BLOCK), 1), float(i == j), 0.0)
            work[rows, PANEL + j * BLOCK : PANEL + (j + 1) * BLOCK] = unit
            factor_t[rows, j * BLOCK : (j + 1) * BLOCK] = jnp.zeros((BLOCK, BLOCK), F32)

    for k in range(4):
        rows = slice(k * BLOCK, (k + 1) * BLOCK)
        carry = [work[k * BLOCK + g * 8 : k * BLOCK + g * 8 + 8, rows] for g in range(16)]
        carry += [
            work[k * BLOCK + g * 8 : k * BLOCK + g * 8 + 8, PANEL + k * BLOCK : PANEL + (k + 1) * BLOCK]
            for g in range(16)
        ]
        d, x = carry[:16], carry[16:]
        for part in range(4):
            n = 16 - 4 * part
            carry = lax.fori_loop(
                part * 4, part * 4 + 4, lambda g, v, n=n: eliminate(g, v, n, diag_f, diag_x), tuple(d + x)
            )
            d, x = list(carry[: n - 4]), list(carry[n : 2 * n - 4])
            if part in (0, 2):
                advance()
        factor_t[rows, rows] = diag_f[...]
        right = (k + 1) * BLOCK
        width = PANEL + (k + 1) * BLOCK - right
        solved = jnp.dot(diag_x[...], work[rows, right : right + width], precision=HIGHEST)
        work[rows, right : right + width] = solved
        count = PANEL - right
        if count:
            factor_t[rows, right:PANEL] = solved[:, :count]
            turned = jnp.transpose(solved[:, :count])
            work[right:PANEL, right : right + width] -= jnp.dot(turned, solved, precision=HIGHEST)

    columns = jnp.concatenate(
        [jnp.concatenate([heads[4 + i, j] for j in range(4)], axis=1) for i in range(2)], axis=0
    )
    solved = lax.dot_general(
        work[:, PANEL:], columns, (((1,), (1,)), ((), ())), precision=HIGHEST, preferred_element_type=F32
    )
    turned = jnp.transpose(work[:, PANEL:])
    weight = jnp.dot(turned, solved, precision=HIGHEST)
    work[:, :PANEL] = turned
    own_panel = col_id < PANEL // BLOCK
    direct = -work[:, pl.ds(pl.multiple_of(jnp.minimum(col_id, 3) * BLOCK, BLOCK), BLOCK)]
    weight = jnp.concatenate([jnp.where(own_panel, direct, weight[:, :BLOCK]), weight[:, BLOCK:]], axis=1)
    high = weight.astype(BF16)
    w_high[...] = high
    w_low[...] = (weight - high.astype(F32)).astype(BF16)
    dot = functools.partial(jnp.dot, preferred_element_type=F32)

    def update(c):
        if c:
            finish2(c)
        start, size = PIECES[c]
        at = slice(start, start + size)
        left_rows = jnp.concatenate([panel[j, at, :] for j in range(4)], axis=1)
        high = left_rows.astype(BF16)
        low = (left_rows - high.astype(F32)).astype(BF16)
        product = dot(high, w_high[...]) + (dot(high, w_low[...]) + dot(low, w_high[...]))
        out[at, :BLOCK] = jnp.where(own_panel, 0.0, a[0, at]) - product[:, :BLOCK]
        out[at, BLOCK:] = a[1, at] - product[:, BLOCK:]
        if c == 0:

            @pl.when(row_id < PANEL // BLOCK)
            def _():
                d, j = jnp.minimum(row_id, 3), jnp.minimum(col_id, 3)
                block = factor_t[
                    pl.ds(pl.multiple_of(j * BLOCK, BLOCK), BLOCK), pl.ds(pl.multiple_of(d * BLOCK, BLOCK), BLOCK)
                ]
                out[:BLOCK, :BLOCK] = jnp.where(own_panel, jnp.transpose(block), a[0, :BLOCK])
                out[:BLOCK, BLOCK:] = a[1, :BLOCK]

    done = 0
    while next2 < NC:
        advance()
        for _ in range(2):
            if done <= next2 - 4:
                update(done)
                done += 1
    while done < NC:
        update(done)
        done += 1

    for c in range(NC):

        @pl.when(left)
        def _(c=c):
            send(own, c, sent0.at[c], got0.at[c], cross).wait_send()

        mate1, j1, mate2, _ = plan(c)
        send(own, c, sent1.at[c], got1.at[c], mate1).wait_send()
        send(own, c, sent2.at[c, 0], got2.at[c, 0], mate2).wait_send()
        send(j1, c, sent2.at[c, 1], got2.at[c, 1], mate2).wait_send()
    head_done()


def panel_step(inverse, weight_a, weight_b, kaula, rows, goce):
    dma = pltpu.SemaphoreType.DMA
    smem, anywhere = pl.BlockSpec(memory_space=pltpu.SMEM), pl.BlockSpec(memory_space=pl.ANY)
    return pl.pallas_call(
        panel_kernel,
        out_shape=jax.ShapeDtypeStruct((RH, CH), F32),
        in_specs=[smem] * 3 + [pl.BlockSpec(memory_space=pltpu.VMEM), anywhere, anywhere],
        out_specs=pl.BlockSpec(memory_space=pltpu.VMEM),
        scratch_shapes=[
            pltpu.VMEM((2 * RH, 128), F32),
            pltpu.VMEM((RH, CH), F32),
            pltpu.VMEM((32, 2, 8, 128), F32),
            pltpu.VMEM((2, RH, BLOCK), F32),
            pltpu.VMEM((4, RH, BLOCK), F32),
            pltpu.VMEM((6, 4, BLOCK, BLOCK), F32),
            pltpu.VMEM((PANEL, 2 * PANEL), F32),
            pltpu.VMEM((PANEL, PANEL), F32),
            pltpu.VMEM((PANEL, CH), BF16),
            pltpu.VMEM((PANEL, CH), BF16),
            pltpu.VMEM((BLOCK, BLOCK), F32),
            pltpu.VMEM((BLOCK, BLOCK), F32),
            dma((2,)),
            dma((NC,)),
            dma((NC,)),
            dma((NC,)),
            dma((NC,)),
            dma((NC, 2)),
            dma((NC, 2)),
            dma((16,)),
            dma((6,)),
        ],
        compiler_params=pltpu.CompilerParams(
            collective_id=0, has_side_effects=True, vmem_limit_bytes=VMEM_LIMIT
        ),
        name="panel_step",
    )(inverse, weight_a, weight_b, kaula.reshape(1, CH), rows, goce)


def shards(grace_slab, goce_slab, grace_weight, goce_weight, kaula_prior, row_target, column_target):
    row_id = lax.axis_index("prow")
    targets = lax.dynamic_slice_in_dim(row_target, row_id * RH, RH)
    targets, order = lax.sort((targets, jnp.arange(RH, dtype=jnp.int32)), num_keys=1)
    places = targets.reshape(NPR, 1, GR) - jnp.arange(NPR, dtype=jnp.int32)[:, None, None] * RH
    split_rows = grace_slab.reshape(RH // 8, 8, 2, 128).transpose(0, 2, 1, 3).reshape(2 * RH, 128)
    rows, inverse = exchange(linear(order), column_target, places, split_rows)
    return panel_step(inverse, grace_weight, goce_weight, kaula_prior, rows.reshape(2 * RH, 128), goce_slab)


def solution(mesh):
    return jax.shard_map(
        shards,
        mesh=mesh,
        in_specs=(P("prow", "pcol"), P("prow", "pcol"), P(), P(), P("pcol"), P(), P()),
        out_specs=P("prow", "pcol"),
        check_vma=False,
    )
```

```python
import functools

import jax
import jax.numpy as jnp
from jax import lax
from jax.experimental import pallas as pl
from jax.experimental.pallas import tpu as pltpu
from jax.sharding import PartitionSpec as P

F32, BF16 = jnp.float32, jnp.bfloat16
MESH = pl.DeviceIdType.MESH
HIGHEST = lax.Precision.HIGHEST
PANEL, BLOCK = 512, 128
NPR, NPC = 16, 8
RH, CH = 5632, 256
GR, GC = RH // NPR, CH // NPC
QR = GR // 4
PIECES = [(0, BLOCK)] + [(at, 256) for at in range(BLOCK, RH - 256, 256)] + [(RH - BLOCK, BLOCK)]
NC = len(PIECES)
VMEM_LIMIT = 60 * 2**20
INV_ROWS = 48


def iota(shape, dim):
    return lax.broadcasted_iota(jnp.int32, shape, dim)


def select_columns(values, onehot):
    high = values.astype(BF16)
    rest = values - high.astype(F32)
    middle = rest.astype(BF16)
    low = (rest - middle.astype(F32)).astype(BF16)
    dot = functools.partial(jnp.dot, preferred_element_type=F32)
    return dot(high, onehot) + dot(middle, onehot) + dot(low, onehot)


def regroup(parts, lane):
    results = []
    for m in range(4):
        joined = None
        for k in range(4):
            moved = parts[k] if k == m else pltpu.roll(parts[k], ((k - m) * GC) % 128, 1)
            joined = moved if k == 0 else jnp.where(lane // GC == k, moved, joined)
        results.append(joined)
    return results


def linear(row):
    return row // 8 * 16 + row % 8


def turn_row(row_id, col_id, step):
    return jnp.bitwise_xor(row_id, lax.rem(step + 2 * col_id, NPR))


def turn_col(row_id, col_id, k):
    return jnp.bitwise_xor(col_id, lax.rem(k + row_id, NPC))


def exchange_kernel(
    order, col_all, places, x, out, inverse_out, pick_in,
    rows, packed, received, places_in, pick_out, sent, got, place_sent, place_got,
):
    row_id, col_id = lax.axis_index("prow"), lax.axis_index("pcol")
    me = row_id * NPC + col_id
    lane = iota((QR, 128), 1)

    barrier = pltpu.get_barrier_semaphore()

    def greet(k, carry):
        to = lax.rem(me + k, NPR * NPC)
        pl.semaphore_signal(barrier, inc=1, device_id=(to // NPC, to % NPC), device_id_type=MESH)
        return carry

    lax.fori_loop(1, NPR * NPC, greet, 0)

    mine = [col_all[pl.ds(col_id * 2 + h, 1), :].astype(F32) for h in range(2)]
    across = jnp.concatenate(mine, axis=1)
    down = jnp.concatenate([jnp.transpose(jnp.broadcast_to(v, (128, 128))) for v in mine], axis=0)
    below = (jnp.concatenate([down, down], axis=1) > across).astype(F32)
    rank = jnp.sum(below, axis=1, keepdims=True).astype(jnp.int32)
    pick_out[...] = jnp.where(rank == iota((CH, CH), 1), 1.0, 0.0).astype(BF16)

    def pack(step):
        dest = turn_row(row_id, col_id, step)
        base = dest * GR

        def gather(i, carry):
            for u in range(16):
                at = order[base + i * 16 + u]
                tile, sub = i * 2 + u // 8, u % 8
                rows[tile, 0, sub : sub + 1, :] = x[pl.ds(at, 1), :]
                rows[tile, 1, sub : sub + 1, :] = x[pl.ds(at + 8, 1), :]
            return carry

        lax.fori_loop(0, GR // 16, gather, 0)
        taken = jnp.concatenate([rows[:, h].reshape(GR, 128) for h in range(2)], axis=1)
        picked = select_columns(taken, pick_out[...])
        for half in range(2):
            parts = [picked[g * QR : (g + 1) * QR, half * 128 : half * 128 + 128] for g in range(4)]
            for q, joined in enumerate(regroup(parts, lane)):
                packed[dest * NPC + half * 4 + q] = joined

    def chunk_copy(row, col):
        other = row * NPC + col
        return pltpu.make_async_remote_copy(
            packed.at[other], received.at[me], sent.at[other], got.at[me],
            device_id=(row, col), device_id_type=MESH,
        )

    def chunk_from(row, col):
        other = row * NPC + col
        return pltpu.make_async_remote_copy(
            packed.at[other], received.at[other], sent.at[other], got.at[other],
            device_id=(row, col), device_id_type=MESH,
        )

    def place_copy(row, slot):
        return pltpu.make_async_remote_copy(
            places.at[row], places_in.at[slot], place_sent.at[row], place_got.at[slot],
            device_id=(row, col_id), device_id_type=MESH,
        )

    def own_copy():
        return pltpu.make_async_copy(packed.at[me], received.at[me], got.at[me])

    def own_places():
        return pltpu.make_async_copy(places.at[row_id], places_in.at[row_id], place_got.at[row_id])

    def each(step, remote, local):
        row = turn_row(row_id, col_id, step)
        for k in range(NPC):
            col = turn_col(row_id, col_id, k)
            inside = (row == row_id) & (col == col_id)

            @pl.when(jnp.logical_not(inside))
            def _(col=col):
                remote(row, col)

            if local is not None:
                pl.when(inside)(local)

    pack(0)
    pl.semaphore_wait(barrier, NPR * NPC - 1)
    own_places().start()

    def announce(k, carry):
        place_copy(jnp.bitwise_xor(row_id, k), row_id).start()
        return carry

    lax.fori_loop(1, NPR, announce, 0)

    def forward(step, carry):
        @pl.when(step < NPR - 1)
        def _():
            pack(step + 1)

        each(step, lambda r, c: chunk_copy(r, c).start(), lambda: own_copy().start())
        return carry

    lax.fori_loop(0, NPR, forward, 0)

    source = jnp.zeros((CH, 128), F32)
    here = col_id * CH + iota((CH, 128), 0)
    for r in range(16):
        source += jnp.where(col_all[r : r + 1, :] == here, float(r // 2), 0.0)
    source = jnp.sum(source, axis=1, keepdims=True)
    across = jnp.transpose(jnp.broadcast_to(source, (CH, 128)))[0:1, :]
    earlier = (source == across) & (iota((CH, CH), 0) < iota((CH, CH), 1))
    rank = jnp.sum(jnp.where(earlier, 1.0, 0.0), axis=0, keepdims=True)
    arrival = (across * GC + rank).astype(jnp.int32)
    pick_in[...] = jnp.where(iota((CH, CH), 0) == arrival, 1.0, 0.0).astype(BF16)

    own_places().wait()

    def places_arrive(k, carry):
        origin = jnp.bitwise_xor(row_id, k)
        place_copy(origin, origin).wait_recv()
        return carry

    lax.fori_loop(1, NPR, places_arrive, 0)

    def invert(origin, total):
        place = places_in[origin]
        number = origin * GR + iota((1, GR), 1)
        high, low = number // 64, number % 64
        down = iota((INV_ROWS, GR), 0) == lax.shift_right_logical(place, 7)
        across = jnp.where(iota((BLOCK, GR), 0) == jnp.bitwise_and(place, 127), 1.0, 0.0).astype(BF16)
        for part, scale in ((high, 64.0), (low, 1.0)):
            values = jnp.where(down, part.astype(F32), 0.0).astype(BF16)
            total = total + scale * lax.dot_general(
                values, across, (((1,), (1,)), ((), ())), preferred_element_type=F32
            )
        return total

    number = lax.fori_loop(0, NPR, invert, jnp.zeros((INV_ROWS, BLOCK), F32)).astype(jnp.int32)
    inverse_out[...] = number + lax.shift_right_logical(number, 3) * 8

    def arrive(step, carry):
        origin = turn_row(row_id, col_id, step)
        each(step, lambda r, c: chunk_from(r, c).wait_recv(), lambda: own_copy().wait())
        halves = [regroup([received[origin * NPC + h * 4 + q] for q in range(4)], lane) for h in range(2)]
        joined = [jnp.concatenate(half, axis=0) for half in halves]
        for h in range(2):
            out[origin, :, h] = joined[h].reshape(GR // 8, 8, 128)
        return carry

    lax.fori_loop(0, NPR, arrive, 0)

    def leave(step, carry):
        each(step, lambda r, c: chunk_copy(r, c).wait_send(), None)
        return carry

    lax.fori_loop(0, NPR, leave, 0)

    def announced(k, carry):
        place_copy(jnp.bitwise_xor(row_id, k), row_id).wait_send()
        return carry

    lax.fori_loop(1, NPR, announced, 0)


def exchange(order, col_all, places, x):
    dma, vmem = pltpu.SemaphoreType.DMA, pl.BlockSpec(memory_space=pltpu.VMEM)
    return pl.pallas_call(
        exchange_kernel,
        out_shape=(
            jax.ShapeDtypeStruct((NPR, GR // 8, 2, 8, 128), F32),
            jax.ShapeDtypeStruct((INV_ROWS, BLOCK), jnp.int32),
            jax.ShapeDtypeStruct((CH, CH), BF16),
        ),
        in_specs=[pl.BlockSpec(memory_space=pltpu.SMEM)] + [vmem] * 3,
        out_specs=(vmem, vmem, vmem),
        scratch_shapes=[
            pltpu.VMEM((GR // 8, 2, 8, 128), F32),
            pltpu.VMEM((NPR * NPC, QR, 128), F32),
            pltpu.VMEM((NPR * NPC, QR, 128), F32),
            pltpu.VMEM((NPR, 1, GR), jnp.int32),
            pltpu.VMEM((CH, CH), BF16),
            dma((NPR * NPC,)),
            dma((NPR * NPC,)),
            dma((NPR,)),
            dma((NPR,)),
        ],
        compiler_params=pltpu.CompilerParams(
            collective_id=1, has_side_effects=True, vmem_limit_bytes=VMEM_LIMIT
        ),
        name="exchange",
    )(order, col_all.reshape(16, 128), places, x)


def across_rows(v, s):
    return jnp.broadcast_to(v[s : s + 1, :], (8, 128))


def across_lanes(v, t):
    return jnp.broadcast_to(v[:, t : t + 1], (8, 128))


def eliminate(group, carry, n, factor_t, inverse):
    d, x = list(carry[:n]), list(carry[n:])
    lane, sub = iota((8, 128), 1), iota((8, 128), 0)
    f_rows, x_rows = jnp.zeros((8, 128), F32), jnp.zeros((8, 128), F32)
    pivots = jnp.ones((8, 128), F32)
    z, zx = d[0], x[0]
    own = [across_lanes(z, t) for t in range(8)]
    for s in range(8):
        here = sub == s
        pivot, row, x_row = across_rows(own[s], s), across_rows(z, s), across_rows(zx, s)
        r = pltpu.reciprocal(pivot, approx=True)
        r = r * (2.0 - pivot * r)
        r = r * (2.0 - pivot * r)
        f_rows, x_rows = jnp.where(here, row, f_rows), jnp.where(here, x_row, x_rows)
        pivots = jnp.where(here, pivot, pivots)
        c = own[s] * r
        z = jnp.where(here, row * r, z - c * row)
        zx = jnp.where(here, x_row * r, zx - c * x_row)
        for t in range(s + 1, 8):
            e = across_rows(own[t], s)
            own[t] = jnp.where(here, e * r, own[t] - c * e)
    q = lax.rsqrt(pivots)
    q = q * (1.5 - 0.5 * pivots * q * q)
    at = pl.ds(pl.multiple_of(group * 8, 8), 8)
    live = (lane < 128 - 8 * group) & (lane >= sub)
    factor_t[at, :] = pltpu.roll(jnp.where(live, f_rows * q, 0.0), group * 8, 1)
    inverse[at, :] = x_rows * q
    z_rows, zx_rows = [across_rows(z, t) for t in range(8)], [across_rows(zx, t) for t in range(8)]
    for i in range(1, n):
        di, xi = d[i], x[i]
        for t in range(8):
            c = across_lanes(d[i], t)
            di = di - c * z_rows[t]
            xi = xi - c * zx_rows[t]
        d[i], x[i] = di, xi
    return tuple([pltpu.roll(v, 120, 1) for v in d[1:] + d[:1]] + x[1:] + x[:1])


def panel_kernel(
    inverse, weight_a, weight_b, kaula, pick, rows_hbm, goce_hbm, out,
    source, goce, raw, a, panel, heads, work, factor_t, w_high, w_low, diag_f, diag_x,
    load, sent0, got0, sent1, got1, sent2, got2, head_sent, head_got,
):
    row_id, col_id = lax.axis_index("prow"), lax.axis_index("pcol")
    cx, cy = col_id // 2, col_id % 2
    cz, cyc = row_id // 4, row_id % 4
    left = cx < 2
    b = jnp.where(left, cx, 3 - cx)
    own = b * 2 + cy
    cross = (row_id, (3 - cx) * 2 + cy)
    x_mate = (row_id, (cx + 1 - 2 * (cx % 2)) * 2 + cy)
    y_mate = (row_id, cx * 2 + 1 - cy)
    over_z = [(lax.rem(cz + k, 4) * 4 + cyc, col_id) for k in (1, 2, 3)]
    core = cyc % 2
    y_near = (cz * 4 + lax.rem(cyc + 2, 4), col_id)
    core_mate = (cz * 4 + cyc + 1 - 2 * core, col_id)

    fetch = [
        pltpu.make_async_copy(rows_hbm, source, load.at[0]),
        pltpu.make_async_copy(goce_hbm, goce, load.at[1]),
    ]
    for copy in fetch:
        copy.start()
    barrier = pltpu.get_barrier_semaphore()
    for device in [cross, x_mate, y_mate, y_near, core_mate] + over_z:
        pl.semaphore_signal(barrier, inc=1, device_id=device, device_id_type=MESH)

    def build(c):
        start, size = PIECES[c]

        def gather(i, carry):
            for u in range(16):
                at = inverse[start // 128 + i // 8, i % 8 * 16 + u]
                tile, sub = i * 2 + u // 8, u % 8
                raw[tile, 0, sub : sub + 1, :] = source[pl.ds(at, 1), :]
                raw[tile, 1, sub : sub + 1, :] = source[pl.ds(at + 8, 1), :]
            return carry

        lax.fori_loop(0, size // 16, gather, 0)
        at = slice(start, start + size)
        arrived = jnp.concatenate([raw[: size // 8, h].reshape(size, BLOCK) for h in range(2)], axis=1)
        moved = select_columns(arrived, pick[...])
        for h in range(2):
            cols = slice(h * BLOCK, (h + 1) * BLOCK)
            block = weight_a[0] * moved[:, cols] + weight_b[0] * goce[at, cols]
            if c == 0:
                diagonal = iota((BLOCK, BLOCK), 0) == iota((BLOCK, BLOCK), 1)
                here = (row_id % NPC == col_id) & (row_id // NPC == h)
                block = block + jnp.where(diagonal & here, kaula[:, cols], 0.0)
            a[h, at] = block
            if h == 0:

                @pl.when(left)
                def _():
                    panel[own, at] = block

    def piece(j, c):
        return panel.at[j, pl.ds(*PIECES[c]), :]

    def send(j, c, sent, got, device):
        return pltpu.make_async_remote_copy(
            piece(j, c), piece(j, c), sent, got, device_id=device, device_id_type=MESH
        )

    flip_x, flip_y = (1 - b) * 2 + cy, b * 2 + 1 - cy
    flip_both = (1 - b) * 2 + 1 - cy

    def plan(c):
        if c % 2 == 0:
            return x_mate, flip_x, y_mate, flip_y
        return y_mate, flip_y, x_mate, flip_x

    def start0(c):
        @pl.when(left)
        def _():
            send(own, c, sent0.at[c], got0.at[c], cross).start()

    def start1(c):
        @pl.when(jnp.logical_not(left))
        def _():
            send(own, c, sent0.at[c], got0.at[c], cross).wait_recv()

        send(own, c, sent1.at[c], got1.at[c], plan(c)[0]).start()

    def start2(c):
        mate1, j1, mate2, _ = plan(c)
        send(j1, c, sent1.at[c], got1.at[c], mate1).wait_recv()
        send(own, c, sent2.at[c, 0], got2.at[c, 0], mate2).start()
        send(j1, c, sent2.at[c, 1], got2.at[c, 1], mate2).start()

    def finish2(c):
        _, _, mate2, j2 = plan(c)
        send(j2, c, sent2.at[c, 0], got2.at[c, 0], mate2).wait_recv()
        send(flip_both, c, sent2.at[c, 1], got2.at[c, 1], mate2).wait_recv()

    head = panel.at[:, pl.ds(0, BLOCK), :]
    a_owner = cyc == col_id % 4
    a_core = core == col_id % 2
    first_z = col_id // 4
    far = lax.rem(cyc + 2, 4)

    def head_local(slot):
        return pltpu.make_async_copy(head, heads.at[slot], head_got.at[slot])

    def head_copy(source, slot, k, device):
        return pltpu.make_async_remote_copy(
            source, heads.at[slot], head_sent.at[k], head_got.at[slot],
            device_id=device, device_id_type=MESH,
        )

    sources = [(cz == 0, cyc, 0), (a_owner & (cz == first_z), 4, 3), (a_owner & (cz == first_z + 2), 5, 6)]

    def head_z():
        for mine, slot, base in sources:

            @pl.when(mine)
            def _(slot=slot, base=base):
                head_local(slot).start()
                for k in range(3):
                    head_copy(head, slot, base + k, over_z[k]).start()

    def to_y(slot, k):
        return head_copy(heads.at[slot], slot, k, y_near)

    def to_core(slot, k):
        return head_copy(heads.at[slot], slot, k, core_mate)

    def head_y():
        head_local(cyc).wait()
        to_y(cyc, 9).start()

        @pl.when(a_owner)
        def _():
            for k, slot in enumerate((4, 5)):
                head_local(slot).wait()
                to_y(slot, 10 + k).start()

    def head_core():
        head_local(far).wait()
        to_core(cyc, 12).start()
        to_core(far, 13).start()

        @pl.when(a_core)
        def _():
            for k, slot in enumerate((4, 5)):

                @pl.when(jnp.logical_not(a_owner))
                def _(slot=slot):
                    head_local(slot).wait()

                to_core(slot, 14 + k).start()

    def head_in():
        head_local(cyc + 1 - 2 * core).wait()
        head_local(lax.rem(cyc + 3 - 2 * core, 4)).wait()

        @pl.when(jnp.logical_not(a_core))
        def _():
            for slot in (4, 5):
                head_local(slot).wait()

    def head_done():
        for mine, slot, base in sources:

            @pl.when(mine)
            def _(slot=slot, base=base):
                for k in range(3):
                    head_copy(head, slot, base + k, over_z[k]).wait_send()

        to_y(cyc, 9).wait_send()
        to_core(cyc, 12).wait_send()
        to_core(far, 13).wait_send()
        for k, slot in enumerate((4, 5)):

            @pl.when(a_owner)
            def _(k=k, slot=slot):
                to_y(slot, 10 + k).wait_send()

            @pl.when(a_core)
            def _(k=k, slot=slot):
                to_core(slot, 14 + k).wait_send()

    next0, next1, next2 = 6, 3, 2

    def push():
        nonlocal next0, next1
        if next0 < NC:
            start0(next0)
        if next1 < NC:
            start1(next1)
        if next0 + 1 < NC:
            build(next0 + 1)
        next0, next1 = next0 + 1, next1 + 1

    def advance():
        nonlocal next2
        if next2 < NC:
            start2(next2)
        next2 += 1
        push()

    for copy in fetch:
        copy.wait()
    build(0)
    pl.semaphore_wait(barrier, 8)
    build(1)
    start0(0)
    build(2)
    start0(1)
    start1(0)
    build(3)
    start0(2)
    start2(0)
    build(4)
    start0(3)
    start1(1)
    finish2(0)
    head_z()
    build(5)
    start0(4)
    start1(2)
    start2(1)
    build(6)
    start0(5)
    advance()
    head_y()
    advance()
    push()
    head_core()
    advance()
    push()
    push()
    head_in()

    lower = iota((BLOCK, BLOCK), 0) >= iota((BLOCK, BLOCK), 1)
    for i in range(4):
        rows = slice(i * BLOCK, (i + 1) * BLOCK)
        for j in range(i):
            block = heads[i, j]
            work[rows, j * BLOCK : (j + 1) * BLOCK] = block
            work[j * BLOCK : (j + 1) * BLOCK, rows] = jnp.transpose(block)
        block = heads[i, i]
        work[rows, rows] = jnp.where(lower, block, jnp.transpose(block))
        for j in range(4):
            unit = jnp.where(iota((BLOCK, BLOCK), 0) == iota((BLOCK, BLOCK), 1), float(i == j), 0.0)
            work[rows, PANEL + j * BLOCK : PANEL + (j + 1) * BLOCK] = unit
            factor_t[rows, j * BLOCK : (j + 1) * BLOCK] = jnp.zeros((BLOCK, BLOCK), F32)

    for k in range(4):
        rows = slice(k * BLOCK, (k + 1) * BLOCK)
        carry = [work[k * BLOCK + g * 8 : k * BLOCK + g * 8 + 8, rows] for g in range(16)]
        carry += [
            work[k * BLOCK + g * 8 : k * BLOCK + g * 8 + 8, PANEL + k * BLOCK : PANEL + (k + 1) * BLOCK]
            for g in range(16)
        ]
        d, x = carry[:16], carry[16:]
        for part in range(4):
            n = 16 - 4 * part
            carry = lax.fori_loop(
                part * 4, part * 4 + 4, lambda g, v, n=n: eliminate(g, v, n, diag_f, diag_x), tuple(d + x)
            )
            d, x = list(carry[: n - 4]), list(carry[n : 2 * n - 4])
            if part in (0, 2):
                advance()
        factor_t[rows, rows] = diag_f[...]
        right = (k + 1) * BLOCK
        width = PANEL + (k + 1) * BLOCK - right
        solved = jnp.dot(diag_x[...], work[rows, right : right + width], precision=HIGHEST)
        work[rows, right : right + width] = solved
        count = PANEL - right
        if count:
            factor_t[rows, right:PANEL] = solved[:, :count]
            turned = jnp.transpose(solved[:, :count])
            work[right:PANEL, right : right + width] -= jnp.dot(turned, solved, precision=HIGHEST)

    columns = jnp.concatenate(
        [jnp.concatenate([heads[4 + i, j] for j in range(4)], axis=1) for i in range(2)], axis=0
    )
    solved = lax.dot_general(
        work[:, PANEL:], columns, (((1,), (1,)), ((), ())), precision=HIGHEST, preferred_element_type=F32
    )
    turned = jnp.transpose(work[:, PANEL:])
    weight = jnp.dot(turned, solved, precision=HIGHEST)
    work[:, :PANEL] = turned
    own_panel = col_id < PANEL // BLOCK
    direct = -work[:, pl.ds(pl.multiple_of(jnp.minimum(col_id, 3) * BLOCK, BLOCK), BLOCK)]
    weight = jnp.concatenate([jnp.where(own_panel, direct, weight[:, :BLOCK]), weight[:, BLOCK:]], axis=1)
    high = weight.astype(BF16)
    w_high[...] = high
    w_low[...] = (weight - high.astype(F32)).astype(BF16)
    dot = functools.partial(jnp.dot, preferred_element_type=F32)

    def update(c):
        if c:
            finish2(c)
        start, size = PIECES[c]
        at = slice(start, start + size)
        left_rows = jnp.concatenate([panel[j, at, :] for j in range(4)], axis=1)
        high = left_rows.astype(BF16)
        low = (left_rows - high.astype(F32)).astype(BF16)
        product = dot(high, w_high[...]) + (dot(high, w_low[...]) + dot(low, w_high[...]))
        out[at, :BLOCK] = jnp.where(own_panel, 0.0, a[0, at]) - product[:, :BLOCK]
        out[at, BLOCK:] = a[1, at] - product[:, BLOCK:]
        if c == 0:

            @pl.when(row_id < PANEL // BLOCK)
            def _():
                d, j = jnp.minimum(row_id, 3), jnp.minimum(col_id, 3)
                block = factor_t[
                    pl.ds(pl.multiple_of(j * BLOCK, BLOCK), BLOCK), pl.ds(pl.multiple_of(d * BLOCK, BLOCK), BLOCK)
                ]
                out[:BLOCK, :BLOCK] = jnp.where(own_panel, jnp.transpose(block), a[0, :BLOCK])
                out[:BLOCK, BLOCK:] = a[1, :BLOCK]

    done = 0
    while next2 < NC:
        advance()
        for _ in range(2):
            if done <= next2 - 4:
                update(done)
                done += 1
    while done < NC:
        update(done)
        done += 1

    for c in range(NC):

        @pl.when(left)
        def _(c=c):
            send(own, c, sent0.at[c], got0.at[c], cross).wait_send()

        mate1, j1, mate2, _ = plan(c)
        send(own, c, sent1.at[c], got1.at[c], mate1).wait_send()
        send(own, c, sent2.at[c, 0], got2.at[c, 0], mate2).wait_send()
        send(j1, c, sent2.at[c, 1], got2.at[c, 1], mate2).wait_send()
    head_done()


def panel_step(inverse, pick, weight_a, weight_b, kaula, rows, goce):
    dma = pltpu.SemaphoreType.DMA
    smem, anywhere = pl.BlockSpec(memory_space=pltpu.SMEM), pl.BlockSpec(memory_space=pl.ANY)
    return pl.pallas_call(
        panel_kernel,
        out_shape=jax.ShapeDtypeStruct((RH, CH), F32),
        in_specs=[smem] * 3 + [pl.BlockSpec(memory_space=pltpu.VMEM)] * 2 + [anywhere] * 2,
        out_specs=pl.BlockSpec(memory_space=pltpu.VMEM),
        scratch_shapes=[
            pltpu.VMEM((2 * RH, 128), F32),
            pltpu.VMEM((RH, CH), F32),
            pltpu.VMEM((32, 2, 8, 128), F32),
            pltpu.VMEM((2, RH, BLOCK), F32),
            pltpu.VMEM((4, RH, BLOCK), F32),
            pltpu.VMEM((6, 4, BLOCK, BLOCK), F32),
            pltpu.VMEM((PANEL, 2 * PANEL), F32),
            pltpu.VMEM((PANEL, PANEL), F32),
            pltpu.VMEM((PANEL, CH), BF16),
            pltpu.VMEM((PANEL, CH), BF16),
            pltpu.VMEM((BLOCK, BLOCK), F32),
            pltpu.VMEM((BLOCK, BLOCK), F32),
            dma((2,)),
            dma((NC,)),
            dma((NC,)),
            dma((NC,)),
            dma((NC,)),
            dma((NC, 2)),
            dma((NC, 2)),
            dma((16,)),
            dma((6,)),
        ],
        compiler_params=pltpu.CompilerParams(
            collective_id=0, has_side_effects=True, vmem_limit_bytes=VMEM_LIMIT
        ),
        name="panel_step",
    )(inverse, weight_a, weight_b, kaula.reshape(1, CH), pick, rows, goce)


def shards(grace_slab, goce_slab, grace_weight, goce_weight, kaula_prior, row_target, column_target):
    row_id = lax.axis_index("prow")
    targets = lax.dynamic_slice_in_dim(row_target, row_id * RH, RH)
    targets, order = lax.sort((targets, jnp.arange(RH, dtype=jnp.int32)), num_keys=1)
    places = targets.reshape(NPR, 1, GR) - jnp.arange(NPR, dtype=jnp.int32)[:, None, None] * RH
    split_rows = grace_slab.reshape(RH // 8, 8, 2, 128).transpose(0, 2, 1, 3).reshape(2 * RH, 128)
    rows, inverse, pick = exchange(linear(order), column_target, places, split_rows)
    rows = rows.reshape(2 * RH, 128)
    return panel_step(inverse, pick, grace_weight, goce_weight, kaula_prior, rows, goce_slab)


def solution(mesh):
    return jax.shard_map(
        shards,
        mesh=mesh,
        in_specs=(P("prow", "pcol"), P("prow", "pcol"), P(), P(), P("pcol"), P(), P()),
        out_specs=P("prow", "pcol"),
        check_vma=False,
    )
```

```python
import functools

import jax
import jax.numpy as jnp
from jax import lax
from jax.experimental import pallas as pl
from jax.experimental.pallas import tpu as pltpu
from jax.sharding import PartitionSpec as P

F32, BF16 = jnp.float32, jnp.bfloat16
MESH = pl.DeviceIdType.MESH
HIGHEST = lax.Precision.HIGHEST
PANEL, BLOCK = 512, 128
NPR, NPC = 16, 8
RH, CH = 5632, 256
GR, GC = RH // NPR, CH // NPC
QR = GR // 4
PIECES = [(0, BLOCK)] + [(at, 256) for at in range(BLOCK, RH - 256, 256)] + [(RH - BLOCK, BLOCK)]
NC = len(PIECES)
VMEM_LIMIT = 62 * 2**20
INV_ROWS = 48


def iota(shape, dim):
    return lax.broadcasted_iota(jnp.int32, shape, dim)


def select_columns(values, onehot):
    high = values.astype(BF16)
    rest = values - high.astype(F32)
    middle = rest.astype(BF16)
    low = (rest - middle.astype(F32)).astype(BF16)
    dot = functools.partial(jnp.dot, preferred_element_type=F32)
    return dot(high, onehot) + dot(middle, onehot) + dot(low, onehot)


def regroup(parts, lane):
    results = []
    for m in range(4):
        joined = None
        for k in range(4):
            moved = parts[k] if k == m else pltpu.roll(parts[k], ((k - m) * GC) % 128, 1)
            joined = moved if k == 0 else jnp.where(lane // GC == k, moved, joined)
        results.append(joined)
    return results


def linear(row):
    return row // 8 * 16 + row % 8


def turn_row(row_id, col_id, step):
    return jnp.bitwise_xor(row_id, lax.rem(step + 2 * col_id, NPR))


def turn_col(row_id, col_id, k):
    return jnp.bitwise_xor(col_id, lax.rem(k + row_id, NPC))


def exchange_part(
    order, col_all, places, x, out, inverse_out, pick_in,
    rows, packed, received, places_in, pick_out, sent, got, place_sent, place_got,
):
    row_id, col_id = lax.axis_index("prow"), lax.axis_index("pcol")
    me = row_id * NPC + col_id
    lane = iota((QR, 128), 1)

    barrier = pltpu.get_barrier_semaphore()

    def greet(k, carry):
        to = lax.rem(me + k, NPR * NPC)
        pl.semaphore_signal(barrier, inc=1, device_id=(to // NPC, to % NPC), device_id_type=MESH)
        return carry

    lax.fori_loop(1, NPR * NPC, greet, 0)

    mine = [col_all[pl.ds(col_id * 2 + h, 1), :].astype(F32) for h in range(2)]
    across = jnp.concatenate(mine, axis=1)
    down = jnp.concatenate([jnp.transpose(jnp.broadcast_to(v, (128, 128))) for v in mine], axis=0)
    below = (jnp.concatenate([down, down], axis=1) > across).astype(F32)
    rank = jnp.sum(below, axis=1, keepdims=True).astype(jnp.int32)
    pick_out[...] = jnp.where(rank == iota((CH, CH), 1), 1.0, 0.0).astype(BF16)

    def pack(step):
        dest = turn_row(row_id, col_id, step)
        base = dest * GR

        def gather(i, carry):
            for u in range(16):
                at = order[base + i * 16 + u]
                tile, sub = i * 2 + u // 8, u % 8
                rows[tile, 0, sub : sub + 1, :] = x[pl.ds(at, 1), :]
                rows[tile, 1, sub : sub + 1, :] = x[pl.ds(at + 8, 1), :]
            return carry

        lax.fori_loop(0, GR // 16, gather, 0)
        taken = jnp.concatenate([rows[:, h].reshape(GR, 128) for h in range(2)], axis=1)
        picked = select_columns(taken, pick_out[...])
        for half in range(2):
            parts = [picked[g * QR : (g + 1) * QR, half * 128 : half * 128 + 128] for g in range(4)]
            for q, joined in enumerate(regroup(parts, lane)):
                packed[dest * NPC + half * 4 + q] = joined

    def chunk_copy(row, col):
        other = row * NPC + col
        return pltpu.make_async_remote_copy(
            packed.at[other], received.at[me], sent.at[other], got.at[me],
            device_id=(row, col), device_id_type=MESH,
        )

    def chunk_from(row, col):
        other = row * NPC + col
        return pltpu.make_async_remote_copy(
            packed.at[other], received.at[other], sent.at[other], got.at[other],
            device_id=(row, col), device_id_type=MESH,
        )

    def place_copy(row, slot):
        return pltpu.make_async_remote_copy(
            places.at[row], places_in.at[slot], place_sent.at[row], place_got.at[slot],
            device_id=(row, col_id), device_id_type=MESH,
        )

    def own_copy():
        return pltpu.make_async_copy(packed.at[me], received.at[me], got.at[me])

    def own_places():
        return pltpu.make_async_copy(places.at[row_id], places_in.at[row_id], place_got.at[row_id])

    def each(step, remote, local):
        row = turn_row(row_id, col_id, step)
        for k in range(NPC):
            col = turn_col(row_id, col_id, k)
            inside = (row == row_id) & (col == col_id)

            @pl.when(jnp.logical_not(inside))
            def _(col=col):
                remote(row, col)

            if local is not None:
                pl.when(inside)(local)

    pack(0)
    pl.semaphore_wait(barrier, NPR * NPC - 1)
    own_places().start()

    def announce(k, carry):
        place_copy(jnp.bitwise_xor(row_id, k), row_id).start()
        return carry

    lax.fori_loop(1, NPR, announce, 0)

    def forward(step, carry):
        @pl.when(step < NPR - 1)
        def _():
            pack(step + 1)

        each(step, lambda r, c: chunk_copy(r, c).start(), lambda: own_copy().start())
        return carry

    lax.fori_loop(0, NPR, forward, 0)

    source = jnp.zeros((CH, 128), F32)
    here = col_id * CH + iota((CH, 128), 0)
    for r in range(16):
        source += jnp.where(col_all[r : r + 1, :] == here, float(r // 2), 0.0)
    source = jnp.sum(source, axis=1, keepdims=True)
    across = jnp.transpose(jnp.broadcast_to(source, (CH, 128)))[0:1, :]
    earlier = (source == across) & (iota((CH, CH), 0) < iota((CH, CH), 1))
    rank = jnp.sum(jnp.where(earlier, 1.0, 0.0), axis=0, keepdims=True)
    arrival = (across * GC + rank).astype(jnp.int32)
    pick_in[...] = jnp.where(iota((CH, CH), 0) == arrival, 1.0, 0.0).astype(BF16)

    own_places().wait()

    def places_arrive(k, carry):
        origin = jnp.bitwise_xor(row_id, k)
        place_copy(origin, origin).wait_recv()
        return carry

    lax.fori_loop(1, NPR, places_arrive, 0)

    def invert(origin, total):
        place = places_in[origin]
        number = origin * GR + iota((1, GR), 1)
        high, low = number // 64, number % 64
        down = iota((INV_ROWS, GR), 0) == lax.shift_right_logical(place, 7)
        across = jnp.where(iota((BLOCK, GR), 0) == jnp.bitwise_and(place, 127), 1.0, 0.0).astype(BF16)
        for part, scale in ((high, 64.0), (low, 1.0)):
            values = jnp.where(down, part.astype(F32), 0.0).astype(BF16)
            total = total + scale * lax.dot_general(
                values, across, (((1,), (1,)), ((), ())), preferred_element_type=F32
            )
        return total

    number = lax.fori_loop(0, NPR, invert, jnp.zeros((INV_ROWS, BLOCK), F32)).astype(jnp.int32)
    inverse_out[...] = jnp.minimum(jnp.maximum(number, 0), RH - 1)

    def arrive(step, carry):
        origin = turn_row(row_id, col_id, step)
        each(step, lambda r, c: chunk_from(r, c).wait_recv(), lambda: own_copy().wait())
        halves = [regroup([received[origin * NPC + h * 4 + q] for q in range(4)], lane) for h in range(2)]
        joined = [jnp.concatenate(half, axis=0) for half in halves]
        for h in range(2):
            out[pl.ds(origin * (GR // 8), GR // 8), h] = joined[h].reshape(GR // 8, 8, 128)
        return carry

    lax.fori_loop(0, NPR, arrive, 0)

    def finish():
        def leave(step, carry):
            each(step, lambda r, c: chunk_copy(r, c).wait_send(), None)
            return carry

        lax.fori_loop(0, NPR, leave, 0)

        def announced(k, carry):
            place_copy(jnp.bitwise_xor(row_id, k), row_id).wait_send()
            return carry

        lax.fori_loop(1, NPR, announced, 0)

    return finish


def across_rows(v, s):
    return jnp.broadcast_to(v[s : s + 1, :], (8, 128))


def across_lanes(v, t):
    return jnp.broadcast_to(v[:, t : t + 1], (8, 128))


def eliminate(group, carry, n, factor_t, inverse):
    d, x = list(carry[:n]), list(carry[n:])
    lane, sub = iota((8, 128), 1), iota((8, 128), 0)
    f_rows, x_rows = jnp.zeros((8, 128), F32), jnp.zeros((8, 128), F32)
    pivots = jnp.ones((8, 128), F32)
    z, zx = d[0], x[0]
    own = [across_lanes(z, t) for t in range(8)]
    for s in range(8):
        here = sub == s
        pivot, row, x_row = across_rows(own[s], s), across_rows(z, s), across_rows(zx, s)
        r = pltpu.reciprocal(pivot, approx=True)
        r = r * (2.0 - pivot * r)
        r = r * (2.0 - pivot * r)
        f_rows, x_rows = jnp.where(here, row, f_rows), jnp.where(here, x_row, x_rows)
        pivots = jnp.where(here, pivot, pivots)
        c = own[s] * r
        z = jnp.where(here, row * r, z - c * row)
        zx = jnp.where(here, x_row * r, zx - c * x_row)
        for t in range(s + 1, 8):
            e = across_rows(own[t], s)
            own[t] = jnp.where(here, e * r, own[t] - c * e)
    q = lax.rsqrt(pivots)
    q = q * (1.5 - 0.5 * pivots * q * q)
    at = pl.ds(pl.multiple_of(group * 8, 8), 8)
    live = (lane < 128 - 8 * group) & (lane >= sub)
    factor_t[at, :] = pltpu.roll(jnp.where(live, f_rows * q, 0.0), group * 8, 1)
    inverse[at, :] = x_rows * q
    z_rows, zx_rows = [across_rows(z, t) for t in range(8)], [across_rows(zx, t) for t in range(8)]
    for i in range(1, n):
        di, xi = d[i], x[i]
        for t in range(8):
            c = across_lanes(d[i], t)
            di = di - c * z_rows[t]
            xi = xi - c * zx_rows[t]
        d[i], x[i] = di, xi
    return tuple([pltpu.roll(v, 120, 1) for v in d[1:] + d[:1]] + x[1:] + x[:1])


def step_kernel(
    order, weight_a, weight_b, kaula, col_all, places, x, goce_hbm, out,
    rows, packed, received, places_in, pick_out, sent, got, place_sent, place_got,
    inverse_vector, inverse, pick, source, goce, raw, a, panel, heads, work, factor_t, w_high, w_low, diag_f, diag_x,
    load, sent0, got0, sent1, got1, sent2, got2, head_sent, head_got,
):
    row_id, col_id = lax.axis_index("prow"), lax.axis_index("pcol")
    cx, cy = col_id // 2, col_id % 2
    cz, cyc = row_id // 4, row_id % 4
    left = cx < 2
    b = jnp.where(left, cx, 3 - cx)
    own = b * 2 + cy
    cross = (row_id, (3 - cx) * 2 + cy)
    x_mate = (row_id, (cx + 1 - 2 * (cx % 2)) * 2 + cy)
    y_mate = (row_id, cx * 2 + 1 - cy)
    over_z = [(lax.rem(cz + k, 4) * 4 + cyc, col_id) for k in (1, 2, 3)]
    core = cyc % 2
    y_near = (cz * 4 + lax.rem(cyc + 2, 4), col_id)
    core_mate = (cz * 4 + cyc + 1 - 2 * core, col_id)

    fetch = pltpu.make_async_copy(goce_hbm, goce, load.at[1])
    fetch.start()
    finish_exchange = exchange_part(
        order, col_all, places, x, source, inverse_vector, pick,
        rows, packed, received, places_in, pick_out, sent, got, place_sent, place_got,
    )
    to_scalars = pltpu.make_async_copy(inverse_vector, inverse, load.at[0])
    to_scalars.start()

    def build(c):
        start, size = PIECES[c]

        def gather(i, carry):
            for u in range(16):
                at = inverse[start // 128 + i // 8, i % 8 * 16 + u]
                tile, sub = i * 2 + u // 8, u % 8
                origin, row = lax.shift_right_logical(at, 3), jnp.bitwise_and(at, 7)
                raw[tile, 0, sub : sub + 1, :] = source[origin, 0, pl.ds(row, 1), :]
                raw[tile, 1, sub : sub + 1, :] = source[origin, 1, pl.ds(row, 1), :]
            return carry

        lax.fori_loop(0, size // 16, gather, 0)
        at = slice(start, start + size)
        arrived = jnp.concatenate([raw[: size // 8, h].reshape(size, BLOCK) for h in range(2)], axis=1)
        moved = select_columns(arrived, pick[...])
        for h in range(2):
            cols = slice(h * BLOCK, (h + 1) * BLOCK)
            block = weight_a[0] * moved[:, cols] + weight_b[0] * goce[at, cols]
            if c == 0:
                diagonal = iota((BLOCK, BLOCK), 0) == iota((BLOCK, BLOCK), 1)
                here = (row_id % NPC == col_id) & (row_id // NPC == h)
                block = block + jnp.where(diagonal & here, kaula[:, cols], 0.0)
            a[h, at] = block
            if h == 0:

                @pl.when(left)
                def _():
                    panel[own, at] = block

    def piece(j, c):
        return panel.at[j, pl.ds(*PIECES[c]), :]

    def send(j, c, sent, got, device):
        return pltpu.make_async_remote_copy(
            piece(j, c), piece(j, c), sent, got, device_id=device, device_id_type=MESH
        )

    flip_x, flip_y = (1 - b) * 2 + cy, b * 2 + 1 - cy
    flip_both = (1 - b) * 2 + 1 - cy

    def plan(c):
        if c % 2 == 0:
            return x_mate, flip_x, y_mate, flip_y
        return y_mate, flip_y, x_mate, flip_x

    def start0(c):
        @pl.when(left)
        def _():
            send(own, c, sent0.at[c], got0.at[c], cross).start()

    def start1(c):
        @pl.when(jnp.logical_not(left))
        def _():
            send(own, c, sent0.at[c], got0.at[c], cross).wait_recv()

        send(own, c, sent1.at[c], got1.at[c], plan(c)[0]).start()

    def start2(c):
        mate1, j1, mate2, _ = plan(c)
        send(j1, c, sent1.at[c], got1.at[c], mate1).wait_recv()
        send(own, c, sent2.at[c, 0], got2.at[c, 0], mate2).start()
        send(j1, c, sent2.at[c, 1], got2.at[c, 1], mate2).start()

    def finish2(c):
        _, _, mate2, j2 = plan(c)
        send(j2, c, sent2.at[c, 0], got2.at[c, 0], mate2).wait_recv()
        send(flip_both, c, sent2.at[c, 1], got2.at[c, 1], mate2).wait_recv()

    head = panel.at[:, pl.ds(0, BLOCK), :]
    a_owner = cyc == col_id % 4
    a_core = core == col_id % 2
    first_z = col_id // 4
    far = lax.rem(cyc + 2, 4)

    def head_local(slot):
        return pltpu.make_async_copy(head, heads.at[slot], head_got.at[slot])

    def head_copy(source, slot, k, device):
        return pltpu.make_async_remote_copy(
            source, heads.at[slot], head_sent.at[k], head_got.at[slot],
            device_id=device, device_id_type=MESH,
        )

    sources = [(cz == 0, cyc, 0), (a_owner & (cz == first_z), 4, 3), (a_owner & (cz == first_z + 2), 5, 6)]

    def head_z():
        for mine, slot, base in sources:

            @pl.when(mine)
            def _(slot=slot, base=base):
                head_local(slot).start()
                for k in range(3):
                    head_copy(head, slot, base + k, over_z[k]).start()

    def to_y(slot, k):
        return head_copy(heads.at[slot], slot, k, y_near)

    def to_core(slot, k):
        return head_copy(heads.at[slot], slot, k, core_mate)

    def head_y():
        head_local(cyc).wait()
        to_y(cyc, 9).start()

        @pl.when(a_owner)
        def _():
            for k, slot in enumerate((4, 5)):
                head_local(slot).wait()
                to_y(slot, 10 + k).start()

    def head_core():
        head_local(far).wait()
        to_core(cyc, 12).start()
        to_core(far, 13).start()

        @pl.when(a_core)
        def _():
            for k, slot in enumerate((4, 5)):

                @pl.when(jnp.logical_not(a_owner))
                def _(slot=slot):
                    head_local(slot).wait()

                to_core(slot, 14 + k).start()

    def head_in():
        head_local(cyc + 1 - 2 * core).wait()
        head_local(lax.rem(cyc + 3 - 2 * core, 4)).wait()

        @pl.when(jnp.logical_not(a_core))
        def _():
            for slot in (4, 5):
                head_local(slot).wait()

    def head_done():
        for mine, slot, base in sources:

            @pl.when(mine)
            def _(slot=slot, base=base):
                for k in range(3):
                    head_copy(head, slot, base + k, over_z[k]).wait_send()

        to_y(cyc, 9).wait_send()
        to_core(cyc, 12).wait_send()
        to_core(far, 13).wait_send()
        for k, slot in enumerate((4, 5)):

            @pl.when(a_owner)
            def _(k=k, slot=slot):
                to_y(slot, 10 + k).wait_send()

            @pl.when(a_core)
            def _(k=k, slot=slot):
                to_core(slot, 14 + k).wait_send()

    next0, next1, next2 = 6, 3, 2

    def push():
        nonlocal next0, next1
        if next0 < NC:
            start0(next0)
        if next1 < NC:
            start1(next1)
        if next0 + 1 < NC:
            build(next0 + 1)
        next0, next1 = next0 + 1, next1 + 1

    def advance():
        nonlocal next2
        if next2 < NC:
            start2(next2)
        next2 += 1
        push()

    to_scalars.wait()
    fetch.wait()
    build(0)
    build(1)
    start0(0)
    build(2)
    start0(1)
    start1(0)
    build(3)
    start0(2)
    start2(0)
    build(4)
    start0(3)
    start1(1)
    finish2(0)
    head_z()
    build(5)
    start0(4)
    start1(2)
    start2(1)
    build(6)
    start0(5)
    advance()
    head_y()
    advance()
    push()
    head_core()
    advance()
    push()
    push()
    head_in()

    lower = iota((BLOCK, BLOCK), 0) >= iota((BLOCK, BLOCK), 1)
    for i in range(4):
        rows = slice(i * BLOCK, (i + 1) * BLOCK)
        for j in range(i):
            block = heads[i, j]
            work[rows, j * BLOCK : (j + 1) * BLOCK] = block
            work[j * BLOCK : (j + 1) * BLOCK, rows] = jnp.transpose(block)
        block = heads[i, i]
        work[rows, rows] = jnp.where(lower, block, jnp.transpose(block))
        for j in range(4):
            unit = jnp.where(iota((BLOCK, BLOCK), 0) == iota((BLOCK, BLOCK), 1), float(i == j), 0.0)
            work[rows, PANEL + j * BLOCK : PANEL + (j + 1) * BLOCK] = unit
            factor_t[rows, j * BLOCK : (j + 1) * BLOCK] = jnp.zeros((BLOCK, BLOCK), F32)

    for k in range(4):
        rows = slice(k * BLOCK, (k + 1) * BLOCK)
        carry = [work[k * BLOCK + g * 8 : k * BLOCK + g * 8 + 8, rows] for g in range(16)]
        carry += [
            work[k * BLOCK + g * 8 : k * BLOCK + g * 8 + 8, PANEL + k * BLOCK : PANEL + (k + 1) * BLOCK]
            for g in range(16)
        ]
        d, x = carry[:16], carry[16:]
        for part in range(4):
            n = 16 - 4 * part
            carry = lax.fori_loop(
                part * 4, part * 4 + 4, lambda g, v, n=n: eliminate(g, v, n, diag_f, diag_x), tuple(d + x)
            )
            d, x = list(carry[: n - 4]), list(carry[n : 2 * n - 4])
            if part in (0, 2):
                advance()
        factor_t[rows, rows] = diag_f[...]
        right = (k + 1) * BLOCK
        width = PANEL + (k + 1) * BLOCK - right
        solved = jnp.dot(diag_x[...], work[rows, right : right + width], precision=HIGHEST)
        work[rows, right : right + width] = solved
        count = PANEL - right
        if count:
            factor_t[rows, right:PANEL] = solved[:, :count]
            turned = jnp.transpose(solved[:, :count])
            work[right:PANEL, right : right + width] -= jnp.dot(turned, solved, precision=HIGHEST)

    columns = jnp.concatenate(
        [jnp.concatenate([heads[4 + i, j] for j in range(4)], axis=1) for i in range(2)], axis=0
    )
    solved = lax.dot_general(
        work[:, PANEL:], columns, (((1,), (1,)), ((), ())), precision=HIGHEST, preferred_element_type=F32
    )
    turned = jnp.transpose(work[:, PANEL:])
    weight = jnp.dot(turned, solved, precision=HIGHEST)
    work[:, :PANEL] = turned
    own_panel = col_id < PANEL // BLOCK
    direct = -work[:, pl.ds(pl.multiple_of(jnp.minimum(col_id, 3) * BLOCK, BLOCK), BLOCK)]
    weight = jnp.concatenate([jnp.where(own_panel, direct, weight[:, :BLOCK]), weight[:, BLOCK:]], axis=1)
    high = weight.astype(BF16)
    w_high[...] = high
    w_low[...] = (weight - high.astype(F32)).astype(BF16)
    dot = functools.partial(jnp.dot, preferred_element_type=F32)

    def update(c):
        if c:
            finish2(c)
        start, size = PIECES[c]
        at = slice(start, start + size)
        left_rows = jnp.concatenate([panel[j, at, :] for j in range(4)], axis=1)
        high = left_rows.astype(BF16)
        low = (left_rows - high.astype(F32)).astype(BF16)
        product = dot(high, w_high[...]) + (dot(high, w_low[...]) + dot(low, w_high[...]))
        out[at, :BLOCK] = jnp.where(own_panel, 0.0, a[0, at]) - product[:, :BLOCK]
        out[at, BLOCK:] = a[1, at] - product[:, BLOCK:]
        if c == 0:

            @pl.when(row_id < PANEL // BLOCK)
            def _():
                d, j = jnp.minimum(row_id, 3), jnp.minimum(col_id, 3)
                block = factor_t[
                    pl.ds(pl.multiple_of(j * BLOCK, BLOCK), BLOCK), pl.ds(pl.multiple_of(d * BLOCK, BLOCK), BLOCK)
                ]
                out[:BLOCK, :BLOCK] = jnp.where(own_panel, jnp.transpose(block), a[0, :BLOCK])
                out[:BLOCK, BLOCK:] = a[1, :BLOCK]

    done = 0
    while next2 < NC:
        advance()
        for _ in range(2):
            if done <= next2 - 4:
                update(done)
                done += 1
    while done < NC:
        update(done)
        done += 1

    for c in range(NC):

        @pl.when(left)
        def _(c=c):
            send(own, c, sent0.at[c], got0.at[c], cross).wait_send()

        mate1, j1, mate2, _ = plan(c)
        send(own, c, sent1.at[c], got1.at[c], mate1).wait_send()
        send(own, c, sent2.at[c, 0], got2.at[c, 0], mate2).wait_send()
        send(j1, c, sent2.at[c, 1], got2.at[c, 1], mate2).wait_send()
    head_done()
    finish_exchange()


def step(order, weight_a, weight_b, kaula, col_all, places, x, goce):
    dma, vmem = pltpu.SemaphoreType.DMA, pl.BlockSpec(memory_space=pltpu.VMEM)
    smem, anywhere = pl.BlockSpec(memory_space=pltpu.SMEM), pl.BlockSpec(memory_space=pl.ANY)
    return pl.pallas_call(
        step_kernel,
        out_shape=jax.ShapeDtypeStruct((RH, CH), F32),
        in_specs=[smem] * 3 + [vmem] * 4 + [anywhere],
        out_specs=pl.BlockSpec(memory_space=pltpu.VMEM),
        scratch_shapes=[
            pltpu.VMEM((GR // 8, 2, 8, 128), F32),
            pltpu.VMEM((NPR * NPC, QR, 128), F32),
            pltpu.VMEM((NPR * NPC, QR, 128), F32),
            pltpu.VMEM((NPR, 1, GR), jnp.int32),
            pltpu.VMEM((CH, CH), BF16),
            dma((NPR * NPC,)),
            dma((NPR * NPC,)),
            dma((NPR,)),
            dma((NPR,)),
            pltpu.VMEM((INV_ROWS, BLOCK), jnp.int32),
            pltpu.SMEM((INV_ROWS, BLOCK), jnp.int32),
            pltpu.VMEM((CH, CH), BF16),
            pltpu.VMEM((RH // 8, 2, 8, 128), F32),
            pltpu.VMEM((RH, CH), F32),
            pltpu.VMEM((32, 2, 8, 128), F32),
            pltpu.VMEM((2, RH, BLOCK), F32),
            pltpu.VMEM((4, RH, BLOCK), F32),
            pltpu.VMEM((6, 4, BLOCK, BLOCK), F32),
            pltpu.VMEM((PANEL, 2 * PANEL), F32),
            pltpu.VMEM((PANEL, PANEL), F32),
            pltpu.VMEM((PANEL, CH), BF16),
            pltpu.VMEM((PANEL, CH), BF16),
            pltpu.VMEM((BLOCK, BLOCK), F32),
            pltpu.VMEM((BLOCK, BLOCK), F32),
            dma((2,)),
            dma((NC,)),
            dma((NC,)),
            dma((NC,)),
            dma((NC,)),
            dma((NC, 2)),
            dma((NC, 2)),
            dma((16,)),
            dma((6,)),
        ],
        compiler_params=pltpu.CompilerParams(
            collective_id=0, has_side_effects=True, vmem_limit_bytes=VMEM_LIMIT
        ),
        name="step",
    )(order, weight_a, weight_b, kaula.reshape(1, CH), col_all.reshape(16, 128), places, x, goce)


def shards(grace_slab, goce_slab, grace_weight, goce_weight, kaula_prior, row_target, column_target):
    row_id = lax.axis_index("prow")
    targets = lax.dynamic_slice_in_dim(row_target, row_id * RH, RH)
    targets, order = lax.sort((targets, jnp.arange(RH, dtype=jnp.int32)), num_keys=1)
    places = targets.reshape(NPR, 1, GR) - jnp.arange(NPR, dtype=jnp.int32)[:, None, None] * RH
    split_rows = grace_slab.reshape(RH // 8, 8, 2, 128).transpose(0, 2, 1, 3).reshape(2 * RH, 128)
    return step(
        linear(order), grace_weight, goce_weight, kaula_prior, column_target, places, split_rows, goce_slab
    )


def solution(mesh):
    return jax.shard_map(
        shards,
        mesh=mesh,
        in_specs=(P("prow", "pcol"), P("prow", "pcol"), P(), P(), P("pcol"), P(), P()),
        out_specs=P("prow", "pcol"),
        check_vma=False,
    )
```

```python
import functools

import jax
import jax.numpy as jnp
from jax import lax
from jax.experimental import pallas as pl
from jax.experimental.pallas import tpu as pltpu
from jax.sharding import PartitionSpec as P

F32, BF16 = jnp.float32, jnp.bfloat16
MESH = pl.DeviceIdType.MESH
HIGHEST = lax.Precision.HIGHEST
PANEL, BLOCK = 512, 128
NPR, NPC = 16, 8
RH, CH = 5632, 256
GR, GC = RH // NPR, CH // NPC
QR = GR // 4
PIECES = [(0, BLOCK)] + [(at, 256) for at in range(BLOCK, RH - 256, 256)] + [(RH - BLOCK, BLOCK)]
NC = len(PIECES)
VMEM_LIMIT = 62 * 2**20
INV_ROWS = 48


def iota(shape, dim):
    return lax.broadcasted_iota(jnp.int32, shape, dim)


def select_columns(values, onehot):
    high = values.astype(BF16)
    rest = values - high.astype(F32)
    middle = rest.astype(BF16)
    low = (rest - middle.astype(F32)).astype(BF16)
    dot = functools.partial(jnp.dot, preferred_element_type=F32)
    return dot(high, onehot) + dot(middle, onehot) + dot(low, onehot)


def regroup(parts, lane):
    results = []
    for m in range(4):
        joined = None
        for k in range(4):
            moved = parts[k] if k == m else pltpu.roll(parts[k], ((k - m) * GC) % 128, 1)
            joined = moved if k == 0 else jnp.where(lane // GC == k, moved, joined)
        results.append(joined)
    return results


def linear(row):
    return row // 8 * 16 + row % 8


def turn_row(row_id, col_id, step):
    return jnp.bitwise_xor(row_id, lax.rem(step + 2 * col_id, NPR))


def turn_col(row_id, col_id, k):
    return jnp.bitwise_xor(col_id, lax.rem(k + row_id, NPC))


def exchange_part(
    order, col_all, places, x, out, inverse_out, pick_in,
    rows, packed, received, places_in, pick_out, sent, got, place_sent, place_got,
):
    row_id, col_id = lax.axis_index("prow"), lax.axis_index("pcol")
    me = row_id * NPC + col_id
    lane = iota((QR, 128), 1)

    barrier = pltpu.get_barrier_semaphore()

    def greet(k, carry):
        to = lax.rem(me + k, NPR * NPC)
        pl.semaphore_signal(barrier, inc=1, device_id=(to // NPC, to % NPC), device_id_type=MESH)
        return carry

    lax.fori_loop(1, NPR * NPC, greet, 0)

    mine = [col_all[pl.ds(col_id * 2 + h, 1), :].astype(F32) for h in range(2)]
    across = jnp.concatenate(mine, axis=1)
    down = jnp.concatenate([jnp.transpose(jnp.broadcast_to(v, (128, 128))) for v in mine], axis=0)
    below = (jnp.concatenate([down, down], axis=1) > across).astype(F32)
    rank = jnp.sum(below, axis=1, keepdims=True).astype(jnp.int32)
    pick_out[...] = jnp.where(rank == iota((CH, CH), 1), 1.0, 0.0).astype(BF16)

    def pack(step):
        dest = turn_row(row_id, col_id, step)
        base = dest * GR

        def gather(i, carry):
            for u in range(16):
                at = order[base + i * 16 + u]
                tile, sub = i * 2 + u // 8, u % 8
                rows[tile, 0, sub : sub + 1, :] = x[pl.ds(at, 1), :]
                rows[tile, 1, sub : sub + 1, :] = x[pl.ds(at + 8, 1), :]
            return carry

        lax.fori_loop(0, GR // 16, gather, 0)
        taken = jnp.concatenate([rows[:, h].reshape(GR, 128) for h in range(2)], axis=1)
        picked = select_columns(taken, pick_out[...])
        for half in range(2):
            parts = [picked[g * QR : (g + 1) * QR, half * 128 : half * 128 + 128] for g in range(4)]
            for q, joined in enumerate(regroup(parts, lane)):
                packed[dest * NPC + half * 4 + q] = joined

    def chunk_copy(row, col):
        other = row * NPC + col
        return pltpu.make_async_remote_copy(
            packed.at[other], received.at[me], sent.at[other], got.at[me],
            device_id=(row, col), device_id_type=MESH,
        )

    def chunk_from(row, col):
        other = row * NPC + col
        return pltpu.make_async_remote_copy(
            packed.at[other], received.at[other], sent.at[other], got.at[other],
            device_id=(row, col), device_id_type=MESH,
        )

    def place_copy(row, slot):
        return pltpu.make_async_remote_copy(
            places.at[row], places_in.at[slot], place_sent.at[row], place_got.at[slot],
            device_id=(row, col_id), device_id_type=MESH,
        )

    def own_copy():
        return pltpu.make_async_copy(packed.at[me], received.at[me], got.at[me])

    def own_places():
        return pltpu.make_async_copy(places.at[row_id], places_in.at[row_id], place_got.at[row_id])

    def each(step, remote, local):
        row = turn_row(row_id, col_id, step)
        for k in range(NPC):
            col = turn_col(row_id, col_id, k)
            inside = (row == row_id) & (col == col_id)

            @pl.when(jnp.logical_not(inside))
            def _(col=col):
                remote(row, col)

            if local is not None:
                pl.when(inside)(local)

    pack(0)
    pl.semaphore_wait(barrier, NPR * NPC - 1)
    own_places().start()

    def announce(k, carry):
        place_copy(jnp.bitwise_xor(row_id, k), row_id).start()
        return carry

    lax.fori_loop(1, NPR, announce, 0)

    def forward(step, carry):
        @pl.when(step < NPR - 1)
        def _():
            pack(step + 1)

        each(step, lambda r, c: chunk_copy(r, c).start(), lambda: own_copy().start())
        return carry

    lax.fori_loop(0, NPR, forward, 0)

    source = jnp.zeros((CH, 128), F32)
    here = col_id * CH + iota((CH, 128), 0)
    for r in range(16):
        source += jnp.where(col_all[r : r + 1, :] == here, float(r // 2), 0.0)
    source = jnp.sum(source, axis=1, keepdims=True)
    across = jnp.transpose(jnp.broadcast_to(source, (CH, 128)))[0:1, :]
    earlier = (source == across) & (iota((CH, CH), 0) < iota((CH, CH), 1))
    rank = jnp.sum(jnp.where(earlier, 1.0, 0.0), axis=0, keepdims=True)
    arrival = (across * GC + rank).astype(jnp.int32)
    pick_in[...] = jnp.where(iota((CH, CH), 0) == arrival, 1.0, 0.0).astype(BF16)

    own_places().wait()

    def places_arrive(k, carry):
        origin = jnp.bitwise_xor(row_id, k)
        place_copy(origin, origin).wait_recv()
        return carry

    lax.fori_loop(1, NPR, places_arrive, 0)

    def invert(origin, total):
        place = places_in[origin]
        number = origin * GR + iota((1, GR), 1)
        high, low = number // 64, number % 64
        down = iota((INV_ROWS, GR), 0) == lax.shift_right_logical(place, 7)
        across = jnp.where(iota((BLOCK, GR), 0) == jnp.bitwise_and(place, 127), 1.0, 0.0).astype(BF16)
        for part, scale in ((high, 64.0), (low, 1.0)):
            values = jnp.where(down, part.astype(F32), 0.0).astype(BF16)
            total = total + scale * lax.dot_general(
                values, across, (((1,), (1,)), ((), ())), preferred_element_type=F32
            )
        return total

    number = lax.fori_loop(0, NPR, invert, jnp.zeros((INV_ROWS, BLOCK), F32)).astype(jnp.int32)
    inverse_out[...] = jnp.minimum(jnp.maximum(number, 0), RH - 1)

    def arrive(step, carry):
        origin = turn_row(row_id, col_id, step)
        each(step, lambda r, c: chunk_from(r, c).wait_recv(), lambda: own_copy().wait())
        halves = [regroup([received[origin * NPC + h * 4 + q] for q in range(4)], lane) for h in range(2)]
        joined = [jnp.concatenate(half, axis=0) for half in halves]
        for h in range(2):
            out[pl.ds(origin * (GR // 8), GR // 8), h] = joined[h].reshape(GR // 8, 8, 128)
        return carry

    lax.fori_loop(0, NPR, arrive, 0)

    def finish():
        def leave(step, carry):
            each(step, lambda r, c: chunk_copy(r, c).wait_send(), None)
            return carry

        lax.fori_loop(0, NPR, leave, 0)

        def announced(k, carry):
            place_copy(jnp.bitwise_xor(row_id, k), row_id).wait_send()
            return carry

        lax.fori_loop(1, NPR, announced, 0)

    return finish


def across_rows(v, s):
    return jnp.broadcast_to(v[s : s + 1, :], (8, 128))


def across_lanes(v, t):
    return jnp.broadcast_to(v[:, t : t + 1], (8, 128))


def eliminate(group, carry, n, factor_t, inverse):
    d, x = list(carry[:n]), list(carry[n:])
    lane, sub = iota((8, 128), 1), iota((8, 128), 0)
    f_rows, x_rows = jnp.zeros((8, 128), F32), jnp.zeros((8, 128), F32)
    pivots = jnp.ones((8, 128), F32)
    z, zx = d[0], x[0]
    own = [across_lanes(z, t) for t in range(8)]
    for s in range(8):
        here = sub == s
        pivot, row, x_row = across_rows(own[s], s), across_rows(z, s), across_rows(zx, s)
        r = pltpu.reciprocal(pivot, approx=True)
        r = r * (2.0 - pivot * r)
        r = r * (2.0 - pivot * r)
        f_rows, x_rows = jnp.where(here, row, f_rows), jnp.where(here, x_row, x_rows)
        pivots = jnp.where(here, pivot, pivots)
        c = own[s] * r
        z = jnp.where(here, row * r, z - c * row)
        zx = jnp.where(here, x_row * r, zx - c * x_row)
        for t in range(s + 1, 8):
            e = across_rows(own[t], s)
            own[t] = jnp.where(here, e * r, own[t] - c * e)
    q = lax.rsqrt(pivots)
    q = q * (1.5 - 0.5 * pivots * q * q)
    at = pl.ds(pl.multiple_of(group * 8, 8), 8)
    live = (lane < 128 - 8 * group) & (lane >= sub)
    factor_t[at, :] = pltpu.roll(jnp.where(live, f_rows * q, 0.0), group * 8, 1)
    inverse[at, :] = x_rows * q
    z_rows, zx_rows = [across_rows(z, t) for t in range(8)], [across_rows(zx, t) for t in range(8)]
    for i in range(1, n):
        di, xi = d[i], x[i]
        for t in range(8):
            c = across_lanes(d[i], t)
            di = di - c * z_rows[t]
            xi = xi - c * zx_rows[t]
        d[i], x[i] = di, xi
    return tuple([pltpu.roll(v, 120, 1) for v in d[1:] + d[:1]] + x[1:] + x[:1])


def step_kernel(
    order, weight_a, weight_b, kaula, col_all, places, x, goce_hbm, out_hbm,
    rows, packed, received, places_in, pick_out, sent, got, place_sent, place_got,
    out, written, inverse_vector, inverse, pick, source, goce, raw, a, panel, heads, work, factor_t, w_high, w_low, diag_f, diag_x,
    load, sent0, got0, sent1, got1, sent2, got2, head_sent, head_got,
):
    row_id, col_id = lax.axis_index("prow"), lax.axis_index("pcol")
    cx, cy = col_id // 2, col_id % 2
    cz, cyc = row_id // 4, row_id % 4
    left = cx < 2
    b = jnp.where(left, cx, 3 - cx)
    own = b * 2 + cy
    cross = (row_id, (3 - cx) * 2 + cy)
    x_mate = (row_id, (cx + 1 - 2 * (cx % 2)) * 2 + cy)
    y_mate = (row_id, cx * 2 + 1 - cy)
    over_z = [(lax.rem(cz + k, 4) * 4 + cyc, col_id) for k in (1, 2, 3)]
    core = cyc % 2
    y_near = (cz * 4 + lax.rem(cyc + 2, 4), col_id)
    core_mate = (cz * 4 + cyc + 1 - 2 * core, col_id)

    fetch = pltpu.make_async_copy(goce_hbm, goce, load.at[1])
    fetch.start()
    finish_exchange = exchange_part(
        order, col_all, places, x, source, inverse_vector, pick,
        rows, packed, received, places_in, pick_out, sent, got, place_sent, place_got,
    )
    to_scalars = pltpu.make_async_copy(inverse_vector, inverse, load.at[0])
    to_scalars.start()

    def build(c):
        start, size = PIECES[c]

        def gather(i, carry):
            for u in range(16):
                at = inverse[start // 128 + i // 8, i % 8 * 16 + u]
                tile, sub = i * 2 + u // 8, u % 8
                origin, row = lax.shift_right_logical(at, 3), jnp.bitwise_and(at, 7)
                raw[tile, 0, sub : sub + 1, :] = source[origin, 0, pl.ds(row, 1), :]
                raw[tile, 1, sub : sub + 1, :] = source[origin, 1, pl.ds(row, 1), :]
            return carry

        lax.fori_loop(0, size // 16, gather, 0)
        at = slice(start, start + size)
        arrived = jnp.concatenate([raw[: size // 8, h].reshape(size, BLOCK) for h in range(2)], axis=1)
        moved = select_columns(arrived, pick[...])
        for h in range(2):
            cols = slice(h * BLOCK, (h + 1) * BLOCK)
            block = weight_a[0] * moved[:, cols] + weight_b[0] * goce[at, cols]
            if c == 0:
                diagonal = iota((BLOCK, BLOCK), 0) == iota((BLOCK, BLOCK), 1)
                here = (row_id % NPC == col_id) & (row_id // NPC == h)
                block = block + jnp.where(diagonal & here, kaula[:, cols], 0.0)
            a[h, at] = block
            if h == 0:

                @pl.when(left)
                def _():
                    panel[own, at] = block

    def piece(j, c):
        return panel.at[j, pl.ds(*PIECES[c]), :]

    def send(j, c, sent, got, device):
        return pltpu.make_async_remote_copy(
            piece(j, c), piece(j, c), sent, got, device_id=device, device_id_type=MESH
        )

    flip_x, flip_y = (1 - b) * 2 + cy, b * 2 + 1 - cy
    flip_both = (1 - b) * 2 + 1 - cy

    def plan(c):
        if c % 2 == 0:
            return x_mate, flip_x, y_mate, flip_y
        return y_mate, flip_y, x_mate, flip_x

    def start0(c):
        @pl.when(left)
        def _():
            send(own, c, sent0.at[c], got0.at[c], cross).start()

    def start1(c):
        @pl.when(jnp.logical_not(left))
        def _():
            send(own, c, sent0.at[c], got0.at[c], cross).wait_recv()

        send(own, c, sent1.at[c], got1.at[c], plan(c)[0]).start()

    def start2(c):
        mate1, j1, mate2, _ = plan(c)
        send(j1, c, sent1.at[c], got1.at[c], mate1).wait_recv()
        send(own, c, sent2.at[c, 0], got2.at[c, 0], mate2).start()
        send(j1, c, sent2.at[c, 1], got2.at[c, 1], mate2).start()

    def finish2(c):
        _, _, mate2, j2 = plan(c)
        send(j2, c, sent2.at[c, 0], got2.at[c, 0], mate2).wait_recv()
        send(flip_both, c, sent2.at[c, 1], got2.at[c, 1], mate2).wait_recv()

    head = panel.at[:, pl.ds(0, BLOCK), :]
    a_owner = cyc == col_id % 4
    a_core = core == col_id % 2
    first_z = col_id // 4
    far = lax.rem(cyc + 2, 4)

    def head_local(slot):
        return pltpu.make_async_copy(head, heads.at[slot], head_got.at[slot])

    def head_copy(source, slot, k, device):
        return pltpu.make_async_remote_copy(
            source, heads.at[slot], head_sent.at[k], head_got.at[slot],
            device_id=device, device_id_type=MESH,
        )

    sources = [(cz == 0, cyc, 0), (a_owner & (cz == first_z), 4, 3), (a_owner & (cz == first_z + 2), 5, 6)]

    def head_z():
        for mine, slot, base in sources:

            @pl.when(mine)
            def _(slot=slot, base=base):
                head_local(slot).start()
                for k in range(3):
                    head_copy(head, slot, base + k, over_z[k]).start()

    def to_y(slot, k):
        return head_copy(heads.at[slot], slot, k, y_near)

    def to_core(slot, k):
        return head_copy(heads.at[slot], slot, k, core_mate)

    def head_y():
        head_local(cyc).wait()
        to_y(cyc, 9).start()

        @pl.when(a_owner)
        def _():
            for k, slot in enumerate((4, 5)):
                head_local(slot).wait()
                to_y(slot, 10 + k).start()

    def head_core():
        head_local(far).wait()
        to_core(cyc, 12).start()
        to_core(far, 13).start()

        @pl.when(a_core)
        def _():
            for k, slot in enumerate((4, 5)):

                @pl.when(jnp.logical_not(a_owner))
                def _(slot=slot):
                    head_local(slot).wait()

                to_core(slot, 14 + k).start()

    def head_in():
        head_local(cyc + 1 - 2 * core).wait()
        head_local(lax.rem(cyc + 3 - 2 * core, 4)).wait()

        @pl.when(jnp.logical_not(a_core))
        def _():
            for slot in (4, 5):
                head_local(slot).wait()

    def head_done():
        for mine, slot, base in sources:

            @pl.when(mine)
            def _(slot=slot, base=base):
                for k in range(3):
                    head_copy(head, slot, base + k, over_z[k]).wait_send()

        to_y(cyc, 9).wait_send()
        to_core(cyc, 12).wait_send()
        to_core(far, 13).wait_send()
        for k, slot in enumerate((4, 5)):

            @pl.when(a_owner)
            def _(k=k, slot=slot):
                to_y(slot, 10 + k).wait_send()

            @pl.when(a_core)
            def _(k=k, slot=slot):
                to_core(slot, 14 + k).wait_send()

    next0, next1, next2 = 6, 3, 2

    def push():
        nonlocal next0, next1
        if next0 < NC:
            start0(next0)
        if next1 < NC:
            start1(next1)
        if next0 + 1 < NC:
            build(next0 + 1)
        next0, next1 = next0 + 1, next1 + 1

    def advance():
        nonlocal next2
        if next2 < NC:
            start2(next2)
        next2 += 1
        push()

    to_scalars.wait()
    fetch.wait()
    build(0)
    build(1)
    start0(0)
    build(2)
    start0(1)
    start1(0)
    build(3)
    start0(2)
    start2(0)
    build(4)
    start0(3)
    start1(1)
    finish2(0)
    head_z()
    build(5)
    start0(4)
    start1(2)
    start2(1)
    build(6)
    start0(5)
    advance()
    head_y()
    advance()
    push()
    head_core()
    advance()
    push()
    push()
    head_in()

    lower = iota((BLOCK, BLOCK), 0) >= iota((BLOCK, BLOCK), 1)
    for i in range(4):
        rows = slice(i * BLOCK, (i + 1) * BLOCK)
        for j in range(i):
            block = heads[i, j]
            work[rows, j * BLOCK : (j + 1) * BLOCK] = block
            work[j * BLOCK : (j + 1) * BLOCK, rows] = jnp.transpose(block)
        block = heads[i, i]
        work[rows, rows] = jnp.where(lower, block, jnp.transpose(block))
        for j in range(4):
            unit = jnp.where(iota((BLOCK, BLOCK), 0) == iota((BLOCK, BLOCK), 1), float(i == j), 0.0)
            work[rows, PANEL + j * BLOCK : PANEL + (j + 1) * BLOCK] = unit
            factor_t[rows, j * BLOCK : (j + 1) * BLOCK] = jnp.zeros((BLOCK, BLOCK), F32)

    for k in range(4):
        rows = slice(k * BLOCK, (k + 1) * BLOCK)
        carry = [work[k * BLOCK + g * 8 : k * BLOCK + g * 8 + 8, rows] for g in range(16)]
        carry += [
            work[k * BLOCK + g * 8 : k * BLOCK + g * 8 + 8, PANEL + k * BLOCK : PANEL + (k + 1) * BLOCK]
            for g in range(16)
        ]
        d, x = carry[:16], carry[16:]
        for part in range(4):
            n = 16 - 4 * part
            carry = lax.fori_loop(
                part * 4, part * 4 + 4, lambda g, v, n=n: eliminate(g, v, n, diag_f, diag_x), tuple(d + x)
            )
            d, x = list(carry[: n - 4]), list(carry[n : 2 * n - 4])
            if part in (0, 2):
                advance()
        factor_t[rows, rows] = diag_f[...]
        right = (k + 1) * BLOCK
        width = PANEL + (k + 1) * BLOCK - right
        solved = jnp.dot(diag_x[...], work[rows, right : right + width], precision=HIGHEST)
        work[rows, right : right + width] = solved
        count = PANEL - right
        if count:
            factor_t[rows, right:PANEL] = solved[:, :count]
            turned = jnp.transpose(solved[:, :count])
            work[right:PANEL, right : right + width] -= jnp.dot(turned, solved, precision=HIGHEST)

    columns = jnp.concatenate(
        [jnp.concatenate([heads[4 + i, j] for j in range(4)], axis=1) for i in range(2)], axis=0
    )
    solved = lax.dot_general(
        work[:, PANEL:], columns, (((1,), (1,)), ((), ())), precision=HIGHEST, preferred_element_type=F32
    )
    turned = jnp.transpose(work[:, PANEL:])
    weight = jnp.dot(turned, solved, precision=HIGHEST)
    work[:, :PANEL] = turned
    own_panel = col_id < PANEL // BLOCK
    direct = -work[:, pl.ds(pl.multiple_of(jnp.minimum(col_id, 3) * BLOCK, BLOCK), BLOCK)]
    weight = jnp.concatenate([jnp.where(own_panel, direct, weight[:, :BLOCK]), weight[:, BLOCK:]], axis=1)
    high = weight.astype(BF16)
    w_high[...] = high
    w_low[...] = (weight - high.astype(F32)).astype(BF16)
    dot = functools.partial(jnp.dot, preferred_element_type=F32)

    def update(c):
        if c:
            finish2(c)
        start, size = PIECES[c]
        at = slice(start, start + size)
        left_rows = jnp.concatenate([panel[j, at, :] for j in range(4)], axis=1)
        high = left_rows.astype(BF16)
        low = (left_rows - high.astype(F32)).astype(BF16)
        product = dot(high, w_high[...]) + (dot(high, w_low[...]) + dot(low, w_high[...]))
        out[at, :BLOCK] = jnp.where(own_panel, 0.0, a[0, at]) - product[:, :BLOCK]
        out[at, BLOCK:] = a[1, at] - product[:, BLOCK:]
        if c == 0:

            @pl.when(row_id < PANEL // BLOCK)
            def _():
                d, j = jnp.minimum(row_id, 3), jnp.minimum(col_id, 3)
                block = factor_t[
                    pl.ds(pl.multiple_of(j * BLOCK, BLOCK), BLOCK), pl.ds(pl.multiple_of(d * BLOCK, BLOCK), BLOCK)
                ]
                out[:BLOCK, :BLOCK] = jnp.where(own_panel, jnp.transpose(block), a[0, :BLOCK])
                out[:BLOCK, BLOCK:] = a[1, :BLOCK]

    def write(c):
        at = pl.ds(*PIECES[c])
        return pltpu.make_async_copy(out.at[at], out_hbm.at[at], written.at[c])

    done = 0
    while next2 < NC:
        advance()
        for _ in range(2):
            if done <= next2 - 4:
                update(done)
                if done:
                    write(done - 1).start()
                done += 1
    while done < NC:
        update(done)
        write(done - 1).start()
        done += 1
    write(NC - 1).start()

    for c in range(NC):

        @pl.when(left)
        def _(c=c):
            send(own, c, sent0.at[c], got0.at[c], cross).wait_send()

        mate1, j1, mate2, _ = plan(c)
        send(own, c, sent1.at[c], got1.at[c], mate1).wait_send()
        send(own, c, sent2.at[c, 0], got2.at[c, 0], mate2).wait_send()
        send(j1, c, sent2.at[c, 1], got2.at[c, 1], mate2).wait_send()
    head_done()
    finish_exchange()
    for c in range(NC):
        write(c).wait()


def step(order, weight_a, weight_b, kaula, col_all, places, x, goce):
    dma, vmem = pltpu.SemaphoreType.DMA, pl.BlockSpec(memory_space=pltpu.VMEM)
    smem, anywhere = pl.BlockSpec(memory_space=pltpu.SMEM), pl.BlockSpec(memory_space=pl.ANY)
    return pl.pallas_call(
        step_kernel,
        out_shape=jax.ShapeDtypeStruct((RH, CH), F32),
        in_specs=[smem] * 3 + [vmem] * 4 + [anywhere],
        out_specs=anywhere,
        scratch_shapes=[
            pltpu.VMEM((GR // 8, 2, 8, 128), F32),
            pltpu.VMEM((NPR * NPC, QR, 128), F32),
            pltpu.VMEM((NPR * NPC, QR, 128), F32),
            pltpu.VMEM((NPR, 1, GR), jnp.int32),
            pltpu.VMEM((CH, CH), BF16),
            dma((NPR * NPC,)),
            dma((NPR * NPC,)),
            dma((NPR,)),
            dma((NPR,)),
            pltpu.VMEM((RH, CH), F32),
            dma((NC,)),
            pltpu.VMEM((INV_ROWS, BLOCK), jnp.int32),
            pltpu.SMEM((INV_ROWS, BLOCK), jnp.int32),
            pltpu.VMEM((CH, CH), BF16),
            pltpu.VMEM((RH // 8, 2, 8, 128), F32),
            pltpu.VMEM((RH, CH), F32),
            pltpu.VMEM((32, 2, 8, 128), F32),
            pltpu.VMEM((2, RH, BLOCK), F32),
            pltpu.VMEM((4, RH, BLOCK), F32),
            pltpu.VMEM((6, 4, BLOCK, BLOCK), F32),
            pltpu.VMEM((PANEL, 2 * PANEL), F32),
            pltpu.VMEM((PANEL, PANEL), F32),
            pltpu.VMEM((PANEL, CH), BF16),
            pltpu.VMEM((PANEL, CH), BF16),
            pltpu.VMEM((BLOCK, BLOCK), F32),
            pltpu.VMEM((BLOCK, BLOCK), F32),
            dma((2,)),
            dma((NC,)),
            dma((NC,)),
            dma((NC,)),
            dma((NC,)),
            dma((NC, 2)),
            dma((NC, 2)),
            dma((16,)),
            dma((6,)),
        ],
        compiler_params=pltpu.CompilerParams(
            collective_id=0, has_side_effects=True, vmem_limit_bytes=VMEM_LIMIT
        ),
        name="step",
    )(order, weight_a, weight_b, kaula.reshape(1, CH), col_all.reshape(16, 128), places, x, goce)


def shards(grace_slab, goce_slab, grace_weight, goce_weight, kaula_prior, row_target, column_target):
    row_id = lax.axis_index("prow")
    targets = lax.dynamic_slice_in_dim(row_target, row_id * RH, RH)
    targets, order = lax.sort((targets, jnp.arange(RH, dtype=jnp.int32)), num_keys=1)
    places = targets.reshape(NPR, 1, GR) - jnp.arange(NPR, dtype=jnp.int32)[:, None, None] * RH
    split_rows = grace_slab.reshape(RH // 8, 8, 2, 128).transpose(0, 2, 1, 3).reshape(2 * RH, 128)
    return step(
        linear(order), grace_weight, goce_weight, kaula_prior, column_target, places, split_rows, goce_slab
    )


def solution(mesh):
    return jax.shard_map(
        shards,
        mesh=mesh,
        in_specs=(P("prow", "pcol"), P("prow", "pcol"), P(), P(), P("pcol"), P(), P()),
        out_specs=P("prow", "pcol"),
        check_vma=False,
    )
```
